32 devices in a mesh: batch: 4 (over x, core), vocab: 8 (over z, y).
Axes of the slice: x: 2, y: 2, z: 4, core: 2. Of those that a mesh axis runs over, the one named last changes fastest.
Arguments:
- logits: float32 [256, 152064], P('batch', 'vocab'), may hold values from -18 to 350
- history: int32 [256, 4096], P('batch', 'vocab'), may hold values from 0 to 152063, as said below
- history_weight: bfloat16 [256, 4096], P('batch', 'vocab'), may hold values from 0.25 to 2
- lengths: int32 [256], P('batch'), may hold values from 1 to 4096
- repetition: float32 [256], P('batch'), may hold values from 1.1 to 2
- frequency: float32 [256], P('batch'), may hold values from 0.05 to 0.5
- presence: float32 [256], P('batch'), may hold values from 0.1 to 1.5
Outputs:
- log_probs: float32 [256, 152064], P('batch', 'vocab')
The draws below stay inside these ranges and needn't reach their ends.
Inputs may be any that keep to these rules, and one draw needn't show every extreme that they name: `history`: split each sequence's positions into 8 aligned blocks of equal length and the vocabulary into 8 equal ranges: within one block at most 128 ids fall in any one range.
All inputs are finite; a program needn't handle non-finite values.
Results may differ from the reference program's by a relative error of at most 0.0003.
Values may be sent and summed in bfloat16 or wider, within the bound.
No kernel may reach another device: no remote copies, remote signals or barrier semaphores. Data moves between devices by JAX's collectives and lax.ppermute only.
A program may use at most 64 MiB of HBM per device.

```python
import math
import jax
import jax.numpy as jnp

V = 152064
HIST = 4096
SEQS = 256
CAP = 128
N_VOCAB = 8


def draw_logits(key, part):
    keys = jax.random.split(jax.random.fold_in(key, 11), 1)
    values = 3.0 * jax.random.truncated_normal(keys[0], -6.0, 6.0, (SEQS, V), jnp.float32)
    return values.astype(jnp.float32)


def draw_history(key, part):
    keys = jax.random.split(jax.random.fold_in(key, 23), 5)
    span = HIST // N_VOCAB
    blocks = SEQS * N_VOCAB
    shard_width = V // N_VOCAB
    pool = N_VOCAB * CAP
    labels = (jnp.arange(pool, dtype=jnp.int32) // CAP).astype(jnp.int32)
    favored = jax.random.randint(keys[0], (blocks,), 0, N_VOCAB)
    shuffles = jax.vmap(lambda k: jax.random.permutation(k, pool))(jax.random.split(keys[1], blocks)).astype(jnp.int32)
    scores = jnp.where(labels[None, :] == favored[:, None], -1, shuffles)
    order = jnp.argsort(scores, axis=1, stable=True)[:, :span]
    chosen = labels[order]
    mixing = jax.vmap(lambda k: jax.random.permutation(k, span))(jax.random.split(keys[2], blocks)).astype(jnp.int32)
    dest = jnp.take_along_axis(chosen, mixing, axis=1)
    local = jax.random.randint(keys[3], (blocks, span), 0, shard_width) * jax.random.randint(keys[4], (blocks, span), 0, shard_width) // shard_width
    ids = (dest * shard_width + local).astype(jnp.int32)
    return ids.reshape(SEQS, HIST)


def place_ends(entries, key, least, high):
    place = [jax.random.randint(jax.random.fold_in(key, axis), (), 0, length) for axis, length in enumerate(entries.shape)]
    longest = entries.shape.index(max(entries.shape))
    beside = place[:longest] + [(place[longest] + 1) % entries.shape[longest]] + place[longest + 1:]
    return entries.at[tuple(place)].set(least).at[tuple(beside)].set(high)


def level_of(own_key, shape, cuts, smallest, largest):
    def one(axis_at, blocks):
        draws = jax.random.uniform(jax.random.fold_in(jax.random.fold_in(own_key, 6), axis_at), (blocks,), jnp.float32, smallest / len(cuts), largest / len(cuts))
        return jnp.repeat(jnp.exp(draws), shape[axis_at] // blocks).reshape((-1,) + (1,) * (len(shape) - axis_at - 1))

    level = one(*cuts[0])
    for cut in cuts[1:]:
        level = level * one(*cut)
    return level


def setup_inputs(seed: int = 0) -> dict:
    arg_keys = jax.random.split(jax.random.key(seed), 8)
    logits = draw_logits(jax.random.fold_in(arg_keys[7], 71), 0)
    history = draw_history(jax.random.fold_in(arg_keys[7], 71), 0)
    history_weight = jnp.clip(jnp.exp(math.log(2.0) - 2.0794415 * jax.random.uniform(arg_keys[2], (SEQS, HIST), jnp.float32) ** level_of(arg_keys[2], (SEQS, HIST), ((0, 4), (1, 8)), -0.2, 0.2)), 0.25, 2.0).astype(jnp.bfloat16)
    lengths = place_ends(jax.random.randint(arg_keys[3], (SEQS,), 1, HIST + 1), jax.random.fold_in(arg_keys[3], 1), 1, HIST).astype(jnp.int32)
    repetition = jnp.clip(jnp.exp(math.log(2.0) - 0.597837 * jax.random.uniform(arg_keys[4], (SEQS,), jnp.float32) ** level_of(arg_keys[4], (SEQS,), ((0, 4),), -0.2, 0.2)), 1.1, 2.0)
    frequency = jnp.clip(0.05 + 0.45 * jax.random.uniform(arg_keys[5], (SEQS,), jnp.float32) ** level_of(arg_keys[5], (SEQS,), ((0, 4),), -0.2, 0.2), 0.05, 0.5)
    presence = jnp.clip(0.1 + 1.4 * jax.random.uniform(arg_keys[6], (SEQS,), jnp.float32) ** level_of(arg_keys[6], (SEQS,), ((0, 4),), -0.2, 0.2), 0.1, 1.5)
    return dict(logits=logits, history=history, history_weight=history_weight, lengths=lengths, repetition=repetition, frequency=frequency, presence=presence)


def reference(logits, history, history_weight, lengths, repetition, frequency, presence):
    seqs = history.shape[0]
    width = logits.shape[1]
    positions = jnp.arange(history.shape[1], dtype=jnp.int32)
    valid = positions[None, :] < lengths[:, None]
    rows = jnp.arange(seqs, dtype=jnp.int32)[:, None] * width
    segment = jnp.where(valid, rows + history, seqs * width).astype(jnp.int32)
    total_segments = seqs * width + 1
    counts = jax.ops.segment_sum(valid.astype(jnp.float32).reshape(-1), segment.reshape(-1), num_segments=total_segments)
    counts = counts[:seqs * width].reshape(seqs, width)
    weights = jnp.where(valid, history_weight.astype(jnp.float32), jnp.float32(0.0))
    weighted = jax.ops.segment_sum(weights.reshape(-1), segment.reshape(-1), num_segments=total_segments)
    weighted = weighted[:seqs * width].reshape(seqs, width)
    seen = counts > 0.5
    scaled = jnp.where(logits > 0, logits / repetition[:, None], logits * repetition[:, None])
    adjusted = jnp.where(seen, scaled, logits) - frequency[:, None] * weighted - presence[:, None] * seen.astype(jnp.float32)
    row_max = jnp.max(adjusted, axis=1, keepdims=True)
    row_total = jnp.sum(jnp.exp(adjusted - row_max), axis=1, keepdims=True)
    return adjusted - row_max - jnp.log(row_total)
```

```python
import functools

import jax
import jax.numpy as jnp
from jax import lax
from jax.experimental import pallas as pl
from jax.experimental.pallas import tpu as pltpu
from jax.sharding import PartitionSpec as P

LANES = 128
CHUNK = 256
FIELD = 16
SCALE = 512.0


def column(row, rows):
    wide = jnp.broadcast_to(row, (rows, rows))
    same = lax.broadcasted_iota(jnp.int32, (rows, rows), 0) == lax.broadcasted_iota(
        jnp.int32, (rows, rows), 1
    )
    return jnp.sum(jnp.where(same, wide, 0.0), axis=1, keepdims=True)


def pack_kernel(
    shards, slots, width, ids_hbm, weight_hbm, lengths_hbm, send_ref, ids_ref, weight_ref, lengths_ref, sem
):
    copies = [
        pltpu.make_async_copy(source, target, sem.at[k])
        for k, (source, target) in enumerate(
            ((ids_hbm, ids_ref), (weight_hbm, weight_ref), (lengths_hbm, lengths_ref))
        )
    ]
    for copy in copies:
        copy.start()
    for copy in copies:
        copy.wait()
    rows, span = ids_ref.shape
    tiles = span // LANES
    first = lax.axis_index("vocab") * span
    ids = ids_ref[...]
    lengths = column(lengths_ref[...].astype(jnp.float32), rows)
    positions = (lax.broadcasted_iota(jnp.int32, (rows, span), 1) + first).astype(jnp.float32)
    valid = positions < lengths
    owner = jnp.zeros_like(ids)
    for shard in range(1, shards):
        owner = owner + (ids >= shard * width).astype(jnp.int32)
    code = (weight_ref[...].astype(jnp.float32) * SCALE).astype(jnp.int32)
    payload = ((ids - owner * width) << FIELD) | code
    owner = jnp.where(valid, owner, -1)
    below = lax.broadcasted_iota(jnp.int32, (LANES, LANES), 0) <= lax.broadcasted_iota(
        jnp.int32, (LANES, LANES), 1
    )
    below = below.astype(jnp.float32).astype(jnp.bfloat16)
    lane = lax.broadcasted_iota(jnp.int32, (rows, LANES), 1)
    last = jnp.full((rows, LANES), LANES - 1, jnp.int32)
    for shard in range(shards):
        mine = jnp.concatenate(
            [(owner[:, t * LANES : (t + 1) * LANES] == shard) for t in range(tiles)], axis=0
        )
        mine = jnp.where(mine, 1.0, 0.0).astype(jnp.bfloat16)
        ranks = jnp.dot(mine, below, preferred_element_type=jnp.float32).astype(jnp.int32)
        word = ranks[:rows]
        for t in range(1, tiles):
            word = word | (ranks[t * rows : (t + 1) * rows] << (8 * t))
        totals = jnp.take_along_axis(word, last, axis=1)
        base = jnp.zeros_like(lane)
        shift = jnp.zeros_like(lane)
        start = totals & 255
        for t in range(1, tiles):
            past = lane >= start
            base = jnp.where(past, start, base)
            shift = jnp.where(past, 8 * t, shift)
            start = start + ((totals >> (8 * t)) & 255)
        wanted = lane - base
        place = jnp.zeros_like(lane)
        step = LANES // 2
        while step:
            seen = (jnp.take_along_axis(word, place + (step - 1), axis=1) >> shift) & 255
            place = jnp.where(seen <= wanted, place + step, place)
            step //= 2
        found = jnp.take_along_axis(payload[:, :LANES], place, axis=1)
        for t in range(1, tiles):
            other = jnp.take_along_axis(payload[:, t * LANES : (t + 1) * LANES], place, axis=1)
            found = jnp.where(shift == 8 * t, other, found)
        found = jnp.where(lane < start, found, 0)
        send_ref[shard] = found[:, :slots]


def tally_kernel(
    width, ordered, got_ref, logits_ref, repetition_ref, frequency_ref, presence_ref, adjusted_ref, stats_ref,
    dense, sums, factors, trips, logits_sem, factor_sem,
):
    blocks, rows, _ = got_ref.shape
    groups = rows // 8
    pairs = blocks // 2
    chunks = -(-width // CHUNK)
    uppers = -(-chunks // 16) * 16

    def load(group):
        part = pl.ds(pl.multiple_of(group * 8, 8), 8)
        return pltpu.make_async_copy(logits_ref.at[part], adjusted_ref.at[part], logits_sem.at[group])

    for group in range(groups):
        load(group).start()
    fetches = [
        pltpu.make_async_copy(ref, factors.at[pl.ds(k, 1)], factor_sem.at[k])
        for k, ref in enumerate((repetition_ref, frequency_ref, presence_ref))
    ]
    for fetch in fetches:
        fetch.start()

    lane = lax.broadcasted_iota(jnp.int32, (8, LANES), 1)
    if ordered:
        ones = jnp.ones((LANES, LANES), jnp.bfloat16)

        def merge(group, carry):
            part = pl.ds(pl.multiple_of(group * 8, 8), 8)
            words = [got_ref[block, part, :] for block in range(blocks)]
            full = jnp.concatenate(words, axis=0) > 0
            count = jnp.dot(
                jnp.where(full, 1.0, 0.0).astype(jnp.bfloat16), ones, preferred_element_type=jnp.float32
            ).astype(jnp.int32)
            starts = [jnp.zeros_like(lane)]
            for block in range(blocks):
                starts.append(starts[-1] + count[block * 8 : block * 8 + 8])
            turned = [
                jnp.take_along_axis(words[block], (lane - starts[block]) & (LANES - 1), axis=1)
                for block in range(blocks)
            ]
            for tile in range(blocks):
                spot = lane + tile * LANES
                value = turned[tile]
                for block in range(tile + 1, blocks):
                    value = jnp.where(spot >= starts[block], turned[block], value)
                dense[tile, part, :] = jnp.where(spot < starts[blocks], value, 0)
            most = jnp.max(starts[blocks])
            trips[group] = (most + 2 * LANES - 1) // (2 * LANES)
            return carry

        lax.fori_loop(0, groups, merge, 0)
    else:
        dense[...] = got_ref[...]
        for group in range(groups):
            trips[group] = pairs

    iota = lax.broadcasted_iota(jnp.int32, (CHUNK, LANES), 0).astype(jnp.float32)
    iota = iota.astype(jnp.bfloat16)
    zero = jnp.zeros((), jnp.bfloat16)
    one = jnp.ones((), jnp.bfloat16)

    def spread(array, row, count):
        piece = jnp.broadcast_to(array[row : row + 1], (16, LANES)).astype(jnp.bfloat16)
        return jnp.concatenate([piece] * (count // 16), axis=0)

    def products(group, pair):
        part = pl.ds(pl.multiple_of(group * 8, 8), 8)
        halves = []
        for half in range(2):
            words = dense[pair * 2 + half, part, :]
            local = words >> FIELD
            halves.append((
                (local >> 8).astype(jnp.float32),
                (local & 255).astype(jnp.float32),
                (words & 0xFFFF).astype(jnp.float32) * (1.0 / SCALE),
            ))
        for row in range(8):
            hot_upper, hot_lower = [], []
            for upper_rows, lower_rows, weight_rows in halves:
                upper = spread(upper_rows, row, uppers)
                lower = spread(lower_rows, row, CHUNK)
                weight = spread(weight_rows, row, CHUNK)
                hot_upper.append(jnp.where(upper == iota[:uppers], one, zero))
                hot_lower.append(jnp.where(lower == iota, weight, zero))
            yield row, lax.dot_general(
                jnp.concatenate(hot_upper, axis=1),
                jnp.concatenate(hot_lower, axis=1),
                (((1,), (1,)), ((), ())),
                preferred_element_type=jnp.float32,
            )

    def tally(group, carry):
        for row, total in products(group, 0):
            for half in range(CHUNK // LANES):
                part = total[:, half * LANES : (half + 1) * LANES]
                sums[group, half, pl.ds(row, uppers, stride=8), :] = part

        def more(pair, carry):
            for row, total in products(group, pair):
                for half in range(CHUNK // LANES):
                    part = total[:, half * LANES : (half + 1) * LANES]
                    sums[group, half, pl.ds(row, uppers, stride=8), :] += part
            return carry

        lax.fori_loop(1, trips[group], more, 0)
        return carry

    lax.fori_loop(0, groups, tally, 0)
    for fetch in fetches:
        fetch.wait()

    def penalize(group, spot):
        row0 = pl.multiple_of(group * 8, 8)
        part = pl.ds(row0, 8)
        here = lax.broadcasted_iota(jnp.int32, (8, rows), 1) == row0 + lax.broadcasted_iota(
            jnp.int32, (8, rows), 0
        )

        def mine(k):
            row = jnp.broadcast_to(factors[k : k + 1, :], (8, rows))
            return jnp.sum(jnp.where(here, row, 0.0), axis=1, keepdims=True)

        repetition, frequency, presence = mine(0), mine(1), mine(2)
        inverse = 1.0 / repetition
        best = jnp.full((8, LANES), -jnp.inf, jnp.float32)
        load(group).wait()
        tiles = -(-width // LANES)
        tail = None
        for tile in range(tiles):
            size = min(LANES, width - tile * LANES)
            columns = pl.ds(tile * LANES, size)
            x = adjusted_ref[part, columns]
            chunk, half = divmod(tile, CHUNK // LANES)
            weighted = sums[group, half, chunk * 8 : chunk * 8 + 8, :size]
            scaled = x * jnp.where(x > 0, inverse, repetition)
            value = jnp.where(weighted > 0, scaled - presence, x) - frequency * weighted
            adjusted_ref[part, columns] = value
            if size == LANES:
                best = jnp.maximum(best, value)
            else:
                tail = jnp.max(value, axis=1, keepdims=True)
        top = jnp.max(best, axis=1, keepdims=True)
        if tail is not None:
            top = jnp.maximum(top, tail)
        total = jnp.zeros((8, LANES), jnp.float32)
        rest = jnp.zeros((8, 1), jnp.float32)
        for tile in range(tiles):
            size = min(LANES, width - tile * LANES)
            value = jnp.exp(adjusted_ref[part, pl.ds(tile * LANES, size)] - top)
            if size == LANES:
                total = total + value
            else:
                rest = jnp.sum(value, axis=1, keepdims=True)
        rest = rest + jnp.sum(total, axis=1, keepdims=True)
        line = lax.broadcasted_iota(jnp.int32, (8, 2 * rows), 1)
        seq = row0 + lax.broadcasted_iota(jnp.int32, (8, 2 * rows), 0)
        return spot + jnp.where(line == seq, top, 0.0) + jnp.where(line == seq + rows, rest, 0.0)

    spot = lax.fori_loop(0, groups, penalize, jnp.zeros((8, 2 * rows), jnp.float32))
    spot = jnp.sum(spot, axis=0, keepdims=True)
    stats_ref[...] = jnp.broadcast_to(spot, stats_ref.shape)


def finish_kernel(adjusted_ref, stats_ref, out_ref, result, sem):
    rows = adjusted_ref.shape[0]
    tops = stats_ref[:, :rows]
    totals = stats_ref[:, rows:]
    top = jnp.max(tops, axis=0, keepdims=True)
    total = jnp.log(jnp.sum(totals * jnp.exp(tops - top), axis=0, keepdims=True))
    top, total = column(top, rows), column(total, rows)
    copies = []
    for group in range(rows // 8):
        part = slice(group * 8, group * 8 + 8)
        result[part, :] = adjusted_ref[part, :] - top[part] - total[part]
        copies.append(pltpu.make_async_copy(result.at[part], out_ref.at[part], sem.at[group]))
        copies[-1].start()
    for copy in copies:
        copy.wait()


def vmem(shape, dtype):
    return pltpu.VMEM(shape, dtype)


def outside(array):
    return pltpu.with_memory_space_constraint(array, pltpu.HBM)


def body(logits, history, history_weight, lengths, repetition, frequency, presence):
    rows, width = logits.shape
    span = history.shape[1]
    shards = lax.axis_size("vocab")
    slots = max(2, 2 * span // shards)
    full = pl.BlockSpec(memory_space=pltpu.VMEM)
    away = pl.BlockSpec(memory_space=pltpu.HBM)
    ordered = slots % LANES == 0
    send = pl.pallas_call(
        functools.partial(pack_kernel, shards, slots, width),
        out_shape=vmem((shards, rows, slots), jnp.int32),
        in_specs=[away] * 3,
        out_specs=full,
        scratch_shapes=[
            vmem((rows, span), jnp.int32),
            vmem((rows, span), jnp.bfloat16),
            vmem((1, rows), jnp.int32),
            pltpu.SemaphoreType.DMA((3,)),
        ],
        compiler_params=pltpu.CompilerParams(vmem_limit_bytes=8 << 20),
        name="pack",
    )(outside(history), outside(history_weight), outside(lengths.reshape(1, rows)))
    got = lax.all_to_all(send, "vocab", split_axis=0, concat_axis=0, tiled=True)
    if ordered:
        got = got.reshape(shards, rows, slots // LANES, LANES).transpose(0, 2, 1, 3)
        got = got.reshape(-1, rows, LANES)
    else:
        got = got.transpose(1, 0, 2).reshape(rows, shards * slots)
        got = jnp.pad(got, ((0, 0), (0, -(shards * slots) % LANES)))
        got = got.reshape(rows, -1, LANES).transpose(1, 0, 2)
    if got.shape[0] % 2:
        got = jnp.pad(got, ((0, 1), (0, 0), (0, 0)))
    groups = rows // 8
    uppers = -(-(-(-width // CHUNK)) // 16) * 16
    adjusted, stats = pl.pallas_call(
        functools.partial(tally_kernel, width, ordered),
        out_shape=(vmem((rows, width), jnp.float32), vmem((shards, 2 * rows), jnp.float32)),
        in_specs=[full] + [away] * 4,
        out_specs=(full, full),
        scratch_shapes=[
            vmem(got.shape, jnp.int32),
            vmem((groups, CHUNK // LANES, uppers * 8, LANES), jnp.float32),
            vmem((3, rows), jnp.float32),
            pltpu.SMEM((groups,), jnp.int32),
            pltpu.SemaphoreType.DMA((groups,)),
            pltpu.SemaphoreType.DMA((3,)),
        ],
        compiler_params=pltpu.CompilerParams(vmem_limit_bytes=24 << 20),
        name="tally",
    )(
        got,
        outside(logits),
        outside(repetition.reshape(1, rows)),
        outside(frequency.reshape(1, rows)),
        outside(presence.reshape(1, rows)),
    )
    stats = lax.all_to_all(stats, "vocab", split_axis=0, concat_axis=0, tiled=True)
    return pl.pallas_call(
        finish_kernel,
        out_shape=jax.ShapeDtypeStruct((rows, width), jnp.float32),
        in_specs=[full, full],
        out_specs=away,
        scratch_shapes=[vmem((rows, width), jnp.float32), pltpu.SemaphoreType.DMA((groups,))],
        compiler_params=pltpu.CompilerParams(vmem_limit_bytes=24 << 20),
        name="finish",
    )(adjusted, stats)


def solution(mesh):
    return jax.shard_map(
        body,
        mesh=mesh,
        in_specs=(
            P("batch", "vocab"),
            P("batch", "vocab"),
            P("batch", "vocab"),
            P("batch"),
            P("batch"),
            P("batch"),
            P("batch"),
        ),
        out_specs=P("batch", "vocab"),
        check_vma=False,
    )
```

```python
import functools

import jax
import jax.numpy as jnp
from jax import lax
from jax.experimental import pallas as pl
from jax.experimental.pallas import tpu as pltpu
from jax.sharding import PartitionSpec as P

LANES = 128
FIRST = 4
SECOND = 5
TOGETHER = 4
CHUNK = 128
HALVES = CHUNK // LANES
LOG2E = 1.4426950408889634
LN2 = 0.6931471805599453
LEAST = 1e-20
FIELD = 16
SCALE = 512.0


def pick(table, place):
    return lax.gather(
        table,
        place[:, :, None],
        lax.GatherDimensionNumbers(
            offset_dims=(),
            collapsed_slice_dims=(1,),
            start_index_map=(1,),
            operand_batching_dims=(0,),
            start_indices_batching_dims=(0,),
        ),
        slice_sizes=(1, 1),
        mode=lax.GatherScatterMode.PROMISE_IN_BOUNDS,
    )


def column(row, rows):
    wide = jnp.broadcast_to(row, (rows, rows))
    same = lax.broadcasted_iota(jnp.int32, (rows, rows), 0) == lax.broadcasted_iota(
        jnp.int32, (rows, rows), 1
    )
    return jnp.sum(jnp.where(same, wide, 0.0), axis=1, keepdims=True)


def pack_kernel(
    shards, slots, width, ids_hbm, weight_hbm, lengths_hbm, send_ref, ids_ref, weight_ref, lengths_ref, sem
):
    copies = [
        pltpu.make_async_copy(source, target, sem.at[k])
        for k, (source, target) in enumerate(
            ((ids_hbm, ids_ref), (weight_hbm, weight_ref), (lengths_hbm, lengths_ref))
        )
    ]
    for copy in copies:
        copy.start()
    for copy in copies:
        copy.wait()
    rows, span = ids_ref.shape
    tiles = span // LANES
    first = lax.axis_index("vocab") * span
    ids = ids_ref[...]
    lengths = column(lengths_ref[...].astype(jnp.float32), rows)
    positions = (lax.broadcasted_iota(jnp.int32, (rows, span), 1) + first).astype(jnp.float32)
    valid = positions < lengths
    owner = jnp.zeros_like(ids)
    for shard in range(1, shards):
        owner = owner + (ids >= shard * width).astype(jnp.int32)
    code = (weight_ref[...].astype(jnp.float32) * SCALE).astype(jnp.int32)
    payload = ((ids - owner * width) << FIELD) | code
    owner = jnp.where(valid, owner, -1)
    payloads = [payload[:, t * LANES : (t + 1) * LANES] for t in range(tiles)]
    below = lax.broadcasted_iota(jnp.int32, (LANES, LANES), 0) <= lax.broadcasted_iota(
        jnp.int32, (LANES, LANES), 1
    )
    below = jnp.where(below, 1.0, 0.0)
    low = min(tiles, 3)
    below = [(below * float(256**t)).astype(jnp.bfloat16) for t in range(low)]
    stacked = jnp.concatenate(below, axis=0)
    lane = lax.broadcasted_iota(jnp.int32, (rows, LANES), 1)
    last = jnp.full((rows, LANES), LANES - 1, jnp.int32)

    def place(shard):
        mine = jnp.where(owner == shard, 1.0, 0.0).astype(jnp.bfloat16)
        word = jnp.dot(
            mine[:, : low * LANES], stacked, preferred_element_type=jnp.float32
        ).astype(jnp.int32)
        for t in range(low, tiles):
            high = jnp.dot(
                mine[:, t * LANES : (t + 1) * LANES], below[0], preferred_element_type=jnp.float32
            )
            word = word | (high.astype(jnp.int32) << (8 * t))
        totals = pick(word, last)
        start = totals & 255
        base = jnp.zeros_like(lane)
        lift = jnp.full_like(lane, 24)
        later = []
        for t in range(1, tiles):
            past = lane >= start
            later.append(past)
            base = jnp.where(past, start, base)
            lift = jnp.where(past, 24 - 8 * t, lift)
            start = start + ((totals >> (8 * t)) & 255)
        limit = ((lane - base) << 24) | 0xFFFFFF
        spot = jnp.full_like(lane, -1)
        step = LANES // 2
        while step:
            probe = spot + step
            spot = jnp.where((pick(word, probe) << lift) <= limit, probe, spot)
            step //= 2
        spot = spot + 1
        found = pick(payloads[0], spot)
        for past, other in zip(later, payloads[1:]):
            found = jnp.where(past, pick(other, spot), found)
        send_ref[shard] = jnp.where(lane < start, found, 0)[:, :slots]

    def some(step, carry):
        for k in range(TOGETHER):
            place(step * TOGETHER + k)
        return carry

    lax.fori_loop(0, shards // TOGETHER, some, 0)


def prepare_kernel(
    logits_hbm, repetition_hbm, frequency_hbm, presence_hbm, plain_hbm, seen_hbm, shift_ref, rate_ref,
    logits, plain_ref, seen_ref, factors, logits_sem, factor_sem, plain_sem, seen_sem,
):
    rows, width = plain_ref.shape
    groups = rows // 8
    tiles = -(-width // LANES)
    loads = [
        pltpu.make_async_copy(
            logits_hbm.at[pl.ds(group * 8, 8)], logits.at[pl.ds(group * 8, 8)], logits_sem.at[group]
        )
        for group in range(groups)
    ]
    fetches = [
        pltpu.make_async_copy(ref, factors.at[pl.ds(k, 1)], factor_sem.at[k])
        for k, ref in enumerate((repetition_hbm, frequency_hbm, presence_hbm))
    ]
    for copy in fetches + loads:
        copy.start()
    for fetch in fetches:
        fetch.wait()
    repetition = column(factors[0:1, :], rows)
    rate_ref[...] = jnp.broadcast_to(column(factors[1:2, :], rows) * LOG2E, rate_ref.shape)
    presence = column(factors[2:3, :], rows) * LOG2E
    above, below = LOG2E / repetition, LOG2E * repetition
    stores = []
    for group in range(groups):
        loads[group].wait()
        part = slice(group * 8, group * 8 + 8)
        best = jnp.full((8, LANES), -jnp.inf, jnp.float32)
        tail = None
        for tile in range(tiles):
            size = min(LANES, width - tile * LANES)
            x = logits[part, tile * LANES : tile * LANES + size]
            if size == LANES:
                best = jnp.maximum(best, x)
            else:
                tail = jnp.max(x, axis=1, keepdims=True)
        top = jnp.max(best, axis=1, keepdims=True)
        if tail is not None:
            top = jnp.maximum(top, tail)
        shift = top * LOG2E
        shift_ref[part, :] = jnp.broadcast_to(shift, (8, shift_ref.shape[1]))
        offset = shift + presence[part]
        over, under = above[part], below[part]
        for tile in range(tiles):
            size = min(LANES, width - tile * LANES)
            columns = slice(tile * LANES, tile * LANES + size)
            x = logits[part, columns]
            plain_ref[part, columns] = x * LOG2E - shift
            seen_ref[part, columns] = x * jnp.where(x > 0, over, under) - offset
        stores.append(pltpu.make_async_copy(plain_ref.at[part], plain_hbm.at[part], plain_sem.at[group]))
        stores.append(pltpu.make_async_copy(seen_ref.at[part], seen_hbm.at[part], seen_sem.at[group]))
        for store in stores[-2:]:
            store.start()
    for store in stores:
        store.wait()


def tally_kernel(
    ordered, got_ref, plain_hbm, seen_hbm, shift_ref, rate_ref, adjusted_ref, stats_ref,
    seen_ref, dense_a, dense_b, sums_a, sums_b, trips, plain_sem, seen_sem,
):
    blocks, rows, _ = got_ref.shape
    width = plain_hbm.shape[1]
    groups = rows // 8
    tiles = -(-width // LANES)
    uppers = -(-(-(-width // CHUNK)) // 16) * 16
    first, second = min(FIRST, blocks), min(SECOND, blocks)
    dense, sums = (dense_a, dense_b), (sums_a, sums_b)

    def rows_of(group):
        return pl.ds(pl.multiple_of(group * 8, 8), 8)

    def loads(group):
        part = rows_of(group)
        return (
            pltpu.make_async_copy(plain_hbm.at[part], adjusted_ref.at[part], plain_sem.at[group]),
            pltpu.make_async_copy(seen_hbm.at[part], seen_ref.at[part], seen_sem.at[group]),
        )

    for group in range(groups):
        for copy in loads(group):
            copy.start()

    lane = lax.broadcasted_iota(jnp.int32, (8, LANES), 1)
    ones = jnp.ones((LANES, LANES), jnp.bfloat16)

    def keep(side, tile, word):
        local = word >> FIELD
        fields = (local // CHUNK, local & (CHUNK - 1), word & 0xFFFF)
        for k, field in enumerate(fields):
            value = field.astype(jnp.float32)
            dense[side][k, pl.ds(tile * 8, 8), :] = value * (1.0 / SCALE) if k == 2 else value

    def merge(group, side):
        words = [got_ref[block, rows_of(group), :] for block in range(blocks)]
        if not ordered:
            for block in range(blocks):
                keep(side, block, words[block])
            trips[side] = blocks
            return
        full = jnp.concatenate(words, axis=0) > 0
        count = jnp.dot(
            jnp.where(full, 1.0, 0.0).astype(jnp.bfloat16), ones, preferred_element_type=jnp.float32
        ).astype(jnp.int32)
        starts = [jnp.zeros_like(lane)]
        for block in range(blocks):
            starts.append(starts[-1] + count[block * 8 : block * 8 + 8])
        turned = [
            pick(words[block], (lane - starts[block]) & (LANES - 1))
            for block in range(blocks)
        ]
        for tile in range(blocks):
            spot = lane + tile * LANES
            value = turned[tile]
            for block in range(tile + 1, blocks):
                value = jnp.where(spot >= starts[block], turned[block], value)
            keep(side, tile, jnp.where(spot < starts[blocks], value, 0))
        trips[side] = (jnp.max(starts[blocks]) + LANES - 1) // LANES

    iota = lax.broadcasted_iota(jnp.int32, (max(CHUNK, uppers), LANES), 0).astype(jnp.float32)
    iota = iota.astype(jnp.bfloat16)
    zero = jnp.zeros((), jnp.bfloat16)
    one = jnp.ones((), jnp.bfloat16)

    def product(side, row, first_tile, count):
        def spread(k, tile, size):
            piece = dense[side][k, pl.ds(tile * 8 + row, 8, stride=0), :]
            piece = jnp.concatenate([piece, piece], axis=0).astype(jnp.bfloat16)
            return jnp.concatenate([piece] * (size // 16), axis=0)

        hot_upper, hot_lower = [], []
        for step in range(count):
            tile = first_tile + step
            hot_upper.append(jnp.where(spread(0, tile, uppers) == iota[:uppers], one, zero))
            hot_lower.append(jnp.where(spread(1, tile, CHUNK) == iota[:CHUNK], spread(2, tile, CHUNK), zero))
        return lax.dot_general(
            jnp.concatenate(hot_upper, axis=1),
            jnp.concatenate(hot_lower, axis=1),
            (((1,), (1,)), ((), ())),
            preferred_element_type=jnp.float32,
        )

    def tally_row(side, row, count):
        total = product(side, row, 0, count)
        for half in range(HALVES):
            part = total[:, half * LANES : (half + 1) * LANES]
            sums[side][half, pl.ds(row, uppers, stride=8), :] = part

    def tally_rest(side):
        def more(tile, carry):
            for row in range(8):
                total = product(side, row, tile, 1)
                for half in range(HALVES):
                    part = total[:, half * LANES : (half + 1) * LANES]
                    sums[side][half, pl.ds(row, uppers, stride=8), :] += part
            return carry

        if blocks > second:
            lax.fori_loop(second, trips[side], more, 0)

    line = lax.broadcasted_iota(jnp.int32, (8, 2 * rows), 1)
    inner = lax.broadcasted_iota(jnp.int32, (8, 2 * rows), 0)

    def place(spot, group, shift, rest):
        seq = group * 8 + inner
        return spot + jnp.where(line == seq, shift, 0.0) + jnp.where(line == seq + rows, rest, 0.0)

    def both(group, side, spot):
        for copy in loads(group):
            copy.wait()
        if second == first:
            return part_of(group, side, spot, first)
        return lax.cond(
            trips[1 - side] > first,
            lambda spot: part_of(group, side, spot, second),
            lambda spot: part_of(group, side, spot, first),
            spot,
        )

    def part_of(group, side, spot, count):
        part = rows_of(group)
        rate = rate_ref[part, :]
        total = jnp.zeros((8, LANES), jnp.float32)
        rest = jnp.zeros((8, 1), jnp.float32)
        share = -(-tiles // 8)
        for row in range(8):
            for tile in range(row * share, min(tiles, (row + 1) * share)):
                size = min(LANES, width - tile * LANES)
                columns = pl.ds(tile * LANES, size)
                chunk, half = divmod(tile, HALVES)
                weighted = sums[side][half, chunk * 8 : chunk * 8 + 8, :size]
                value = jnp.where(
                    weighted > 0, seen_ref[part, columns] - rate[:, :size] * weighted, adjusted_ref[part, columns]
                )
                adjusted_ref[part, columns] = value
                value = jnp.exp2(value)
                if size == LANES:
                    total = total + value
                else:
                    rest = jnp.sum(value, axis=1, keepdims=True)
            if count:
                tally_row(1 - side, row, count)
        rest = rest + jnp.sum(total, axis=1, keepdims=True)
        return place(spot, group, shift_ref[part, :], rest)

    def renew(group, spot):
        part = rows_of(group)
        value = adjusted_ref[part, :]
        top = jnp.max(value, axis=1, keepdims=True)
        rest = jnp.sum(jnp.exp2(value - top), axis=1, keepdims=True)
        return place(spot, group, shift_ref[part, :] + top, rest)

    merge(0, 0)
    merge(1, 1)
    for row in range(8):
        tally_row(0, row, second)
    tally_rest(0)

    def two(pair, spot):
        for side in range(2):
            group = pair * 2 + side
            spot = both(group, side, spot)
            tally_rest(1 - side)
            merge(group + 2, side)
        return spot

    empty = jnp.zeros((8, 2 * rows), jnp.float32)
    spot = lax.fori_loop(0, groups // 2 - 1, two, empty)
    spot = both(groups - 2, 0, spot)
    tally_rest(1)
    for copy in loads(groups - 1):
        copy.wait()
    spot = part_of(groups - 1, 1, spot, 0)
    spot = jnp.sum(spot, axis=0, keepdims=True)
    stats_ref[...] = jnp.broadcast_to(spot, stats_ref.shape)

    @pl.when(jnp.min(jnp.where(line[:1] < rows, 1.0, spot)) < LEAST)
    def _():
        exact = jnp.sum(lax.fori_loop(0, groups, renew, empty), axis=0, keepdims=True)
        stats_ref[...] = jnp.broadcast_to(exact, stats_ref.shape)


def finish_kernel(adjusted_ref, shift_ref, stats_ref, out_ref, result, sem):
    rows = adjusted_ref.shape[0]
    tops = stats_ref[:, :rows]
    totals = stats_ref[:, rows:]
    top = jnp.max(tops, axis=0, keepdims=True)
    total = jnp.sum(totals * jnp.exp2(tops - top), axis=0, keepdims=True)
    offset = shift_ref[:, :1] - column(top, rows)
    offset = offset * LN2 - column(jnp.log(total), rows)
    copies = []
    for group in range(rows // 8):
        part = slice(group * 8, group * 8 + 8)
        result[part, :] = adjusted_ref[part, :] * LN2 + offset[part]
        copies.append(pltpu.make_async_copy(result.at[part], out_ref.at[part], sem.at[group]))
        copies[-1].start()
    for copy in copies:
        copy.wait()


def vmem(shape, dtype):
    return pltpu.VMEM(shape, dtype)


def outside(array):
    return pltpu.with_memory_space_constraint(array, pltpu.HBM)


def body(logits, history, history_weight, lengths, repetition, frequency, presence):
    rows, width = logits.shape
    span = history.shape[1]
    shards = lax.axis_size("vocab")
    slots = max(2, 2 * span // shards)
    full = pl.BlockSpec(memory_space=pltpu.VMEM)
    away = pl.BlockSpec(memory_space=pltpu.HBM)
    ordered = slots % LANES == 0
    send = pl.pallas_call(
        functools.partial(pack_kernel, shards, slots, width),
        out_shape=vmem((shards, rows, slots), jnp.int32),
        in_specs=[away] * 3,
        out_specs=full,
        scratch_shapes=[
            vmem((rows, span), jnp.int32),
            vmem((rows, span), jnp.bfloat16),
            vmem((1, rows), jnp.int32),
            pltpu.SemaphoreType.DMA((3,)),
        ],
        compiler_params=pltpu.CompilerParams(vmem_limit_bytes=8 << 20),
        name="pack",
    )(outside(history), outside(history_weight), outside(lengths.reshape(1, rows)))
    got = lax.all_to_all(send, "vocab", split_axis=0, concat_axis=0, tiled=True)
    if ordered:
        got = got.reshape(shards, rows, slots // LANES, LANES).transpose(0, 2, 1, 3)
        got = got.reshape(-1, rows, LANES)
    else:
        got = got.transpose(1, 0, 2).reshape(rows, shards * slots)
        got = jnp.pad(got, ((0, 0), (0, -(shards * slots) % LANES)))
        got = got.reshape(rows, -1, LANES).transpose(1, 0, 2)
    got = jnp.pad(got, ((0, got.shape[0] % 2), (0, 0), (0, 0)))
    groups = rows // 8
    uppers = -(-(-(-width // CHUNK)) // 16) * 16
    wide = vmem((rows, width), jnp.float32)
    plain, seen, shift, rate = pl.pallas_call(
        prepare_kernel,
        out_shape=(
            pltpu.HBM((rows, width), jnp.float32),
            pltpu.HBM((rows, width), jnp.float32),
            vmem((rows, 2 * rows), jnp.float32),
            vmem((rows, LANES), jnp.float32),
        ),
        in_specs=[away] * 4,
        out_specs=(away, away, full, full),
        scratch_shapes=[
            wide,
            wide,
            wide,
            vmem((3, rows), jnp.float32),
            pltpu.SemaphoreType.DMA((groups,)),
            pltpu.SemaphoreType.DMA((3,)),
            pltpu.SemaphoreType.DMA((groups,)),
            pltpu.SemaphoreType.DMA((groups,)),
        ],
        compiler_params=pltpu.CompilerParams(vmem_limit_bytes=24 << 20),
        cost_estimate=pl.CostEstimate(
            flops=400 * rows * width, bytes_accessed=400 * rows * width, transcendentals=0
        ),
        name="prepare",
    )(
        outside(logits),
        outside(repetition.reshape(1, rows)),
        outside(frequency.reshape(1, rows)),
        outside(presence.reshape(1, rows)),
    )
    adjusted, stats = pl.pallas_call(
        functools.partial(tally_kernel, ordered),
        out_shape=(wide, vmem((shards, 2 * rows), jnp.float32)),
        in_specs=[full, away, away, full, full],
        out_specs=(full, full),
        scratch_shapes=[
            wide,
            *[vmem((3, got.shape[0] * 8, LANES), jnp.float32)] * 2,
            *[vmem((HALVES, uppers * 8, LANES), jnp.float32)] * 2,
            pltpu.SMEM((2,), jnp.int32),
            pltpu.SemaphoreType.DMA((groups,)),
            pltpu.SemaphoreType.DMA((groups,)),
        ],
        compiler_params=pltpu.CompilerParams(vmem_limit_bytes=16 << 20),
        name="tally",
    )(got, outside(plain), outside(seen), shift, rate)
    stats = lax.all_to_all(stats, "vocab", split_axis=0, concat_axis=0, tiled=True)
    return pl.pallas_call(
        finish_kernel,
        out_shape=jax.ShapeDtypeStruct((rows, width), jnp.float32),
        in_specs=[full] * 3,
        out_specs=away,
        scratch_shapes=[wide, pltpu.SemaphoreType.DMA((groups,))],
        compiler_params=pltpu.CompilerParams(vmem_limit_bytes=16 << 20),
        name="finish",
    )(adjusted, shift, stats)


def solution(mesh):
    return jax.shard_map(
        body,
        mesh=mesh,
        in_specs=(
            P("batch", "vocab"),
            P("batch", "vocab"),
            P("batch", "vocab"),
            P("batch"),
            P("batch"),
            P("batch"),
            P("batch"),
        ),
        out_specs=P("batch", "vocab"),
        check_vma=False,
    )
```

```python
import functools

import jax
import jax.numpy as jnp
from jax import lax
from jax.experimental import pallas as pl
from jax.experimental.pallas import tpu as pltpu
from jax.sharding import PartitionSpec as P

LANES = 128
FIRST = 4
SECOND = 5
TOGETHER = 4
CHUNK = 128
HALVES = CHUNK // LANES
LOG2E = 1.4426950408889634
LN2 = 0.6931471805599453
LEAST = 1e-20
FIELD = 16
SCALE = 512.0


def pick(table, place):
    return lax.gather(
        table,
        place[:, :, None],
        lax.GatherDimensionNumbers(
            offset_dims=(),
            collapsed_slice_dims=(1,),
            start_index_map=(1,),
            operand_batching_dims=(0,),
            start_indices_batching_dims=(0,),
        ),
        slice_sizes=(1, 1),
        mode=lax.GatherScatterMode.PROMISE_IN_BOUNDS,
    )


def column(row, rows):
    wide = jnp.broadcast_to(row, (rows, rows))
    same = lax.broadcasted_iota(jnp.int32, (rows, rows), 0) == lax.broadcasted_iota(
        jnp.int32, (rows, rows), 1
    )
    return jnp.sum(jnp.where(same, wide, 0.0), axis=1, keepdims=True)


def pack_kernel(
    shards, slots, width, ids_hbm, weight_hbm, lengths_hbm, send_ref, ids_ref, weight_ref, lengths_ref, sem
):
    copies = [
        pltpu.make_async_copy(source, target, sem.at[k])
        for k, (source, target) in enumerate(
            ((ids_hbm, ids_ref), (weight_hbm, weight_ref), (lengths_hbm, lengths_ref))
        )
    ]
    for copy in copies:
        copy.start()
    for copy in copies:
        copy.wait()
    rows, span = ids_ref.shape
    tiles = span // LANES
    first = lax.axis_index("vocab") * span
    ids = ids_ref[...]
    lengths = column(lengths_ref[...].astype(jnp.float32), rows)
    positions = (lax.broadcasted_iota(jnp.int32, (rows, span), 1) + first).astype(jnp.float32)
    valid = positions < lengths
    owner = jnp.zeros_like(ids)
    for shard in range(1, shards):
        owner = owner + (ids >= shard * width).astype(jnp.int32)
    code = (weight_ref[...].astype(jnp.float32) * SCALE).astype(jnp.int32)
    payload = ((ids - owner * width) << FIELD) | code
    owner = jnp.where(valid, owner, -1)
    payloads = [payload[:, t * LANES : (t + 1) * LANES] for t in range(tiles)]
    below = lax.broadcasted_iota(jnp.int32, (LANES, LANES), 0) <= lax.broadcasted_iota(
        jnp.int32, (LANES, LANES), 1
    )
    below = jnp.where(below, 1.0, 0.0)
    low = min(tiles, 3)
    below = [(below * float(256**t)).astype(jnp.bfloat16) for t in range(low)]
    stacked = jnp.concatenate(below, axis=0)
    lane = lax.broadcasted_iota(jnp.int32, (rows, LANES), 1)
    last = jnp.full((rows, LANES), LANES - 1, jnp.int32)

    def place(shard):
        mine = jnp.where(owner == shard, 1.0, 0.0).astype(jnp.bfloat16)
        word = jnp.dot(
            mine[:, : low * LANES], stacked, preferred_element_type=jnp.float32
        ).astype(jnp.int32)
        for t in range(low, tiles):
            high = jnp.dot(
                mine[:, t * LANES : (t + 1) * LANES], below[0], preferred_element_type=jnp.float32
            )
            word = word | (high.astype(jnp.int32) << (8 * t))
        totals = pick(word, last)
        start = totals & 255
        base = jnp.zeros_like(lane)
        lift = jnp.full_like(lane, 24)
        later = []
        for t in range(1, tiles):
            past = lane >= start
            later.append(past)
            base = jnp.where(past, start, base)
            lift = jnp.where(past, 24 - 8 * t, lift)
            start = start + ((totals >> (8 * t)) & 255)
        limit = ((lane - base) << 24) | 0xFFFFFF
        spot = jnp.full_like(lane, -1)
        step = LANES // 2
        while step:
            probe = spot + step
            spot = jnp.where((pick(word, probe) << lift) <= limit, probe, spot)
            step //= 2
        spot = spot + 1
        found = pick(payloads[0], spot)
        for past, other in zip(later, payloads[1:]):
            found = jnp.where(past, pick(other, spot), found)
        send_ref[shard] = jnp.where(lane < start, found, 0)[:, :slots]

    def some(step, carry):
        for k in range(TOGETHER):
            place(step * TOGETHER + k)
        return carry

    lax.fori_loop(0, shards // TOGETHER, some, 0)


def prepare_kernel(
    logits_hbm, repetition_hbm, frequency_hbm, presence_hbm, plain_hbm, seen_hbm, shift_ref, rate_ref,
    logits, plain_ref, seen_ref, factors, logits_sem, factor_sem, plain_sem, seen_sem,
):
    rows, width = plain_ref.shape
    groups = rows // 8
    tiles = -(-width // LANES)
    loads = [
        pltpu.make_async_copy(
            logits_hbm.at[pl.ds(group * 8, 8)], logits.at[pl.ds(group * 8, 8)], logits_sem.at[group]
        )
        for group in range(groups)
    ]
    fetches = [
        pltpu.make_async_copy(ref, factors.at[pl.ds(k, 1)], factor_sem.at[k])
        for k, ref in enumerate((repetition_hbm, frequency_hbm, presence_hbm))
    ]
    for copy in fetches + loads:
        copy.start()
    for fetch in fetches:
        fetch.wait()
    repetition = column(factors[0:1, :], rows)
    rate_ref[...] = jnp.broadcast_to(column(factors[1:2, :], rows) * LOG2E, rate_ref.shape)
    presence = column(factors[2:3, :], rows) * LOG2E
    above, below = LOG2E / repetition, LOG2E * repetition
    stores = []
    for group in range(groups):
        loads[group].wait()
        part = slice(group * 8, group * 8 + 8)
        best = jnp.full((8, LANES), -jnp.inf, jnp.float32)
        tail = None
        for tile in range(tiles):
            size = min(LANES, width - tile * LANES)
            x = logits[part, tile * LANES : tile * LANES + size]
            if size == LANES:
                best = jnp.maximum(best, x)
            else:
                tail = jnp.max(x, axis=1, keepdims=True)
        top = jnp.max(best, axis=1, keepdims=True)
        if tail is not None:
            top = jnp.maximum(top, tail)
        shift = top * LOG2E
        shift_ref[part, :] = jnp.broadcast_to(shift, (8, shift_ref.shape[1]))
        offset = shift + presence[part]
        over, under = above[part], below[part]
        for tile in range(tiles):
            size = min(LANES, width - tile * LANES)
            columns = slice(tile * LANES, tile * LANES + size)
            x = logits[part, columns]
            plain_ref[part, columns] = x * LOG2E - shift
            seen_ref[part, columns] = x * jnp.where(x > 0, over, under) - offset
        stores.append(pltpu.make_async_copy(plain_ref.at[part], plain_hbm.at[part], plain_sem.at[group]))
        stores.append(pltpu.make_async_copy(seen_ref.at[part], seen_hbm.at[part], seen_sem.at[group]))
        for store in stores[-2:]:
            store.start()
    for store in stores:
        store.wait()


def tally_kernel(
    ordered, got_ref, plain_hbm, seen_hbm, shift_ref, rate_ref, adjusted_ref, stats_ref,
    seen_ref, dense_a, dense_b, sums_a, sums_b, trips, plain_sem, seen_sem,
):
    blocks, rows, _ = got_ref.shape
    width = plain_hbm.shape[1]
    groups = rows // 8
    tiles = -(-width // LANES)
    uppers = -(-(-(-width // CHUNK)) // 16) * 16
    first, second = min(FIRST, blocks), min(SECOND, blocks)
    dense, sums = (dense_a, dense_b), (sums_a, sums_b)

    def rows_of(group):
        return pl.ds(pl.multiple_of(group * 8, 8), 8)

    def loads(group):
        part = rows_of(group)
        return (
            pltpu.make_async_copy(plain_hbm.at[part], adjusted_ref.at[part], plain_sem.at[group]),
            pltpu.make_async_copy(seen_hbm.at[part], seen_ref.at[part], seen_sem.at[group]),
        )

    for group in range(groups):
        for copy in loads(group):
            copy.start()

    lane = lax.broadcasted_iota(jnp.int32, (8, LANES), 1)
    ones = jnp.ones((LANES, LANES), jnp.bfloat16)

    def keep(side, tile, word):
        local = word >> FIELD
        fields = (local // CHUNK, local & (CHUNK - 1), word & 0xFFFF)
        for k, field in enumerate(fields):
            value = field.astype(jnp.float32)
            dense[side][k, pl.ds(tile * 8, 8), :] = value * (1.0 / SCALE) if k == 2 else value

    def merge(group, side):
        words = [got_ref[block, rows_of(group), :] for block in range(blocks)]
        if not ordered:
            for block in range(blocks):
                keep(side, block, words[block])
            trips[side] = blocks
            return
        full = jnp.concatenate(words, axis=0) > 0
        count = jnp.dot(
            jnp.where(full, 1.0, 0.0).astype(jnp.bfloat16), ones, preferred_element_type=jnp.float32
        ).astype(jnp.int32)
        starts = [jnp.zeros_like(lane)]
        for block in range(blocks):
            starts.append(starts[-1] + count[block * 8 : block * 8 + 8])
        turned = [
            pick(words[block], (lane - starts[block]) & (LANES - 1))
            for block in range(blocks)
        ]
        for tile in range(blocks):
            spot = lane + tile * LANES
            value = turned[tile]
            for block in range(tile + 1, blocks):
                value = jnp.where(spot >= starts[block], turned[block], value)
            keep(side, tile, jnp.where(spot < starts[blocks], value, 0))
        trips[side] = (jnp.max(starts[blocks]) + LANES - 1) // LANES

    iota = lax.broadcasted_iota(jnp.int32, (max(CHUNK, uppers), LANES), 0).astype(jnp.float32)
    iota = iota.astype(jnp.bfloat16)
    zero = jnp.zeros((), jnp.bfloat16)
    one = jnp.ones((), jnp.bfloat16)

    def product(side, row, first_tile, count):
        def spread(k, tile, size):
            piece = dense[side][k, pl.ds(tile * 8 + row, 8, stride=0), :]
            piece = jnp.concatenate([piece, piece], axis=0).astype(jnp.bfloat16)
            return jnp.concatenate([piece] * (size // 16), axis=0)

        hot_upper, hot_lower = [], []
        for step in range(count):
            tile = first_tile + step
            hot_upper.append(jnp.where(spread(0, tile, uppers) == iota[:uppers], one, zero))
            hot_lower.append(jnp.where(spread(1, tile, CHUNK) == iota[:CHUNK], spread(2, tile, CHUNK), zero))
        return lax.dot_general(
            jnp.concatenate(hot_upper, axis=1),
            jnp.concatenate(hot_lower, axis=1),
            (((1,), (1,)), ((), ())),
            preferred_element_type=jnp.float32,
        )

    def tally_row(side, row, count):
        total = product(side, row, 0, count)
        for half in range(HALVES):
            part = total[:, half * LANES : (half + 1) * LANES]
            sums[side][half, pl.ds(row, uppers, stride=8), :] = part

    def tally_rest(side):
        def more(tile, carry):
            for row in range(8):
                total = product(side, row, tile, 1)
                for half in range(HALVES):
                    part = total[:, half * LANES : (half + 1) * LANES]
                    sums[side][half, pl.ds(row, uppers, stride=8), :] += part
            return carry

        if blocks > second:
            lax.fori_loop(second, trips[side], more, 0)

    line = lax.broadcasted_iota(jnp.int32, (8, 2 * rows), 1)
    inner = lax.broadcasted_iota(jnp.int32, (8, 2 * rows), 0)

    def place(spot, group, shift, rest):
        seq = group * 8 + inner
        return spot + jnp.where(line == seq, shift, 0.0) + jnp.where(line == seq + rows, rest, 0.0)

    def both(group, side, spot, following=None):
        for copy in loads(group):
            copy.wait()
        return either(1 - side, lambda count: part_of(group, side, spot, count, following))

    def either(side, run):
        if second == first:
            return run(first)
        return lax.cond(trips[side] > first, lambda: run(second), lambda: run(first))

    def part_of(group, side, spot, count, following):
        if following is not None:
            merge(following, side)
        part = rows_of(group)
        rate = rate_ref[part, :]
        total = jnp.zeros((8, LANES), jnp.float32)
        rest = jnp.zeros((8, 1), jnp.float32)
        share = -(-tiles // 8)
        for row in range(8):
            for tile in range(row * share, min(tiles, (row + 1) * share)):
                size = min(LANES, width - tile * LANES)
                columns = pl.ds(tile * LANES, size)
                chunk, half = divmod(tile, HALVES)
                weighted = sums[side][half, chunk * 8 : chunk * 8 + 8, :size]
                value = jnp.where(
                    weighted > 0, seen_ref[part, columns] - rate[:, :size] * weighted, adjusted_ref[part, columns]
                )
                adjusted_ref[part, columns] = value
                value = jnp.exp2(value)
                if size == LANES:
                    total = total + value
                else:
                    rest = jnp.sum(value, axis=1, keepdims=True)
            if count:
                tally_row(1 - side, row, count)
        rest = rest + jnp.sum(total, axis=1, keepdims=True)
        return place(spot, group, shift_ref[part, :], rest)

    def renew(group, spot):
        part = rows_of(group)
        value = adjusted_ref[part, :]
        top = jnp.max(value, axis=1, keepdims=True)
        rest = jnp.sum(jnp.exp2(value - top), axis=1, keepdims=True)
        return place(spot, group, shift_ref[part, :] + top, rest)

    def begin(count):
        merge(1, 1)
        for row in range(8):
            tally_row(0, row, count)

    merge(0, 0)
    either(0, begin)
    tally_rest(0)

    def two(pair, spot):
        for side in range(2):
            group = pair * 2 + side
            spot = both(group, side, spot, group + 2)
            tally_rest(1 - side)
        return spot

    empty = jnp.zeros((8, 2 * rows), jnp.float32)
    spot = lax.fori_loop(0, groups // 2 - 1, two, empty)
    spot = both(groups - 2, 0, spot)
    tally_rest(1)
    for copy in loads(groups - 1):
        copy.wait()
    spot = part_of(groups - 1, 1, spot, 0, None)
    spot = jnp.sum(spot, axis=0, keepdims=True)
    stats_ref[...] = jnp.broadcast_to(spot, stats_ref.shape)

    @pl.when(jnp.min(jnp.where(line[:1] < rows, 1.0, spot)) < LEAST)
    def _():
        exact = jnp.sum(lax.fori_loop(0, groups, renew, empty), axis=0, keepdims=True)
        stats_ref[...] = jnp.broadcast_to(exact, stats_ref.shape)


def finish_kernel(adjusted_ref, shift_ref, stats_ref, out_ref, result, sem):
    rows = adjusted_ref.shape[0]
    tops = stats_ref[:, :rows]
    totals = stats_ref[:, rows:]
    top = jnp.max(tops, axis=0, keepdims=True)
    total = jnp.sum(totals * jnp.exp2(tops - top), axis=0, keepdims=True)
    offset = shift_ref[:, :1] - column(top, rows)
    offset = offset * LN2 - column(jnp.log(total), rows)
    copies = []
    for group in range(rows // 8):
        part = slice(group * 8, group * 8 + 8)
        result[part, :] = adjusted_ref[part, :] * LN2 + offset[part]
        copies.append(pltpu.make_async_copy(result.at[part], out_ref.at[part], sem.at[group]))
        copies[-1].start()
    for copy in copies:
        copy.wait()


def vmem(shape, dtype):
    return pltpu.VMEM(shape, dtype)


def outside(array):
    return pltpu.with_memory_space_constraint(array, pltpu.HBM)


def body(logits, history, history_weight, lengths, repetition, frequency, presence):
    rows, width = logits.shape
    span = history.shape[1]
    shards = lax.axis_size("vocab")
    slots = max(2, 2 * span // shards)
    full = pl.BlockSpec(memory_space=pltpu.VMEM)
    away = pl.BlockSpec(memory_space=pltpu.HBM)
    ordered = slots % LANES == 0
    send = pl.pallas_call(
        functools.partial(pack_kernel, shards, slots, width),
        out_shape=vmem((shards, rows, slots), jnp.int32),
        in_specs=[away] * 3,
        out_specs=full,
        scratch_shapes=[
            vmem((rows, span), jnp.int32),
            vmem((rows, span), jnp.bfloat16),
            vmem((1, rows), jnp.int32),
            pltpu.SemaphoreType.DMA((3,)),
        ],
        compiler_params=pltpu.CompilerParams(vmem_limit_bytes=8 << 20),
        name="pack",
    )(outside(history), outside(history_weight), outside(lengths.reshape(1, rows)))
    got = lax.all_to_all(send, "vocab", split_axis=0, concat_axis=0, tiled=True)
    if ordered:
        got = got.reshape(shards, rows, slots // LANES, LANES).transpose(0, 2, 1, 3)
        got = got.reshape(-1, rows, LANES)
    else:
        got = got.transpose(1, 0, 2).reshape(rows, shards * slots)
        got = jnp.pad(got, ((0, 0), (0, -(shards * slots) % LANES)))
        got = got.reshape(rows, -1, LANES).transpose(1, 0, 2)
    got = jnp.pad(got, ((0, got.shape[0] % 2), (0, 0), (0, 0)))
    groups = rows // 8
    uppers = -(-(-(-width // CHUNK)) // 16) * 16
    wide = vmem((rows, width), jnp.float32)
    plain, seen, shift, rate = pl.pallas_call(
        prepare_kernel,
        out_shape=(
            pltpu.HBM((rows, width), jnp.float32),
            pltpu.HBM((rows, width), jnp.float32),
            vmem((rows, 2 * rows), jnp.float32),
            vmem((rows, LANES), jnp.float32),
        ),
        in_specs=[away] * 4,
        out_specs=(away, away, full, full),
        scratch_shapes=[
            wide,
            wide,
            wide,
            vmem((3, rows), jnp.float32),
            pltpu.SemaphoreType.DMA((groups,)),
            pltpu.SemaphoreType.DMA((3,)),
            pltpu.SemaphoreType.DMA((groups,)),
            pltpu.SemaphoreType.DMA((groups,)),
        ],
        compiler_params=pltpu.CompilerParams(vmem_limit_bytes=24 << 20),
        cost_estimate=pl.CostEstimate(
            flops=400 * rows * width, bytes_accessed=400 * rows * width, transcendentals=0
        ),
        name="prepare",
    )(
        outside(logits),
        outside(repetition.reshape(1, rows)),
        outside(frequency.reshape(1, rows)),
        outside(presence.reshape(1, rows)),
    )
    adjusted, stats = pl.pallas_call(
        functools.partial(tally_kernel, ordered),
        out_shape=(wide, vmem((shards, 2 * rows), jnp.float32)),
        in_specs=[full, away, away, full, full],
        out_specs=(full, full),
        scratch_shapes=[
            wide,
            *[vmem((3, got.shape[0] * 8, LANES), jnp.float32)] * 2,
            *[vmem((HALVES, uppers * 8, LANES), jnp.float32)] * 2,
            pltpu.SMEM((2,), jnp.int32),
            pltpu.SemaphoreType.DMA((groups,)),
            pltpu.SemaphoreType.DMA((groups,)),
        ],
        compiler_params=pltpu.CompilerParams(vmem_limit_bytes=16 << 20),
        name="tally",
    )(got, outside(plain), outside(seen), shift, rate)
    stats = lax.all_to_all(stats, "vocab", split_axis=0, concat_axis=0, tiled=True)
    return pl.pallas_call(
        finish_kernel,
        out_shape=jax.ShapeDtypeStruct((rows, width), jnp.float32),
        in_specs=[full] * 3,
        out_specs=away,
        scratch_shapes=[wide, pltpu.SemaphoreType.DMA((groups,))],
        compiler_params=pltpu.CompilerParams(vmem_limit_bytes=16 << 20),
        name="finish",
    )(adjusted, shift, stats)


def solution(mesh):
    return jax.shard_map(
        body,
        mesh=mesh,
        in_specs=(
            P("batch", "vocab"),
            P("batch", "vocab"),
            P("batch", "vocab"),
            P("batch"),
            P("batch"),
            P("batch"),
            P("batch"),
        ),
        out_specs=P("batch", "vocab"),
        check_vma=False,
    )
```

```python
import functools

import jax
import jax.numpy as jnp
from jax import lax
from jax.experimental import pallas as pl
from jax.experimental.pallas import tpu as pltpu
from jax.sharding import PartitionSpec as P

LANES = 128
PROFILE = (2, 2, 3, 3, 4, 4, 4, 5)
TOGETHER = 4
CHUNK = 128
HALVES = CHUNK // LANES
LOG2E = 1.4426950408889634
LN2 = 0.6931471805599453
LEAST = 1e-20
FIELD = 16
SCALE = 512.0


def pick(table, place):
    return lax.gather(
        table,
        place[:, :, None],
        lax.GatherDimensionNumbers(
            offset_dims=(),
            collapsed_slice_dims=(1,),
            start_index_map=(1,),
            operand_batching_dims=(0,),
            start_indices_batching_dims=(0,),
        ),
        slice_sizes=(1, 1),
        mode=lax.GatherScatterMode.PROMISE_IN_BOUNDS,
    )


def column(row, rows):
    wide = jnp.broadcast_to(row, (rows, rows))
    same = lax.broadcasted_iota(jnp.int32, (rows, rows), 0) == lax.broadcasted_iota(
        jnp.int32, (rows, rows), 1
    )
    return jnp.sum(jnp.where(same, wide, 0.0), axis=1, keepdims=True)


def pack_kernel(
    shards, slots, width, ids_hbm, weight_hbm, lengths_hbm, send_ref, ids_ref, weight_ref, lengths_ref, sem
):
    copies = [
        pltpu.make_async_copy(source, target, sem.at[k])
        for k, (source, target) in enumerate(
            ((ids_hbm, ids_ref), (weight_hbm, weight_ref), (lengths_hbm, lengths_ref))
        )
    ]
    for copy in copies:
        copy.start()
    for copy in copies:
        copy.wait()
    rows, span = ids_ref.shape
    tiles = span // LANES
    first = lax.axis_index("vocab") * span
    ids = ids_ref[...]
    lengths = column(lengths_ref[...].astype(jnp.float32), rows)
    positions = (lax.broadcasted_iota(jnp.int32, (rows, span), 1) + first).astype(jnp.float32)
    valid = positions < lengths
    owner = jnp.zeros_like(ids)
    for shard in range(1, shards):
        owner = owner + (ids >= shard * width).astype(jnp.int32)
    code = (weight_ref[...].astype(jnp.float32) * SCALE).astype(jnp.int32)
    payload = ((ids - owner * width) << FIELD) | code
    owner = jnp.where(valid, owner, -1)
    payloads = [payload[:, t * LANES : (t + 1) * LANES] for t in range(tiles)]
    below = lax.broadcasted_iota(jnp.int32, (LANES, LANES), 0) <= lax.broadcasted_iota(
        jnp.int32, (LANES, LANES), 1
    )
    below = jnp.where(below, 1.0, 0.0)
    low = min(tiles, 3)
    below = [(below * float(256**t)).astype(jnp.bfloat16) for t in range(low)]
    stacked = jnp.concatenate(below, axis=0)
    lane = lax.broadcasted_iota(jnp.int32, (rows, LANES), 1)
    last = jnp.full((rows, LANES), LANES - 1, jnp.int32)

    def place(shard):
        mine = jnp.where(owner == shard, 1.0, 0.0).astype(jnp.bfloat16)
        word = jnp.dot(
            mine[:, : low * LANES], stacked, preferred_element_type=jnp.float32
        ).astype(jnp.int32)
        for t in range(low, tiles):
            high = jnp.dot(
                mine[:, t * LANES : (t + 1) * LANES], below[0], preferred_element_type=jnp.float32
            )
            word = word | (high.astype(jnp.int32) << (8 * t))
        totals = pick(word, last)
        start = totals & 255
        base = jnp.zeros_like(lane)
        lift = jnp.full_like(lane, 24)
        later = []
        for t in range(1, tiles):
            past = lane >= start
            later.append(past)
            base = jnp.where(past, start, base)
            lift = jnp.where(past, 24 - 8 * t, lift)
            start = start + ((totals >> (8 * t)) & 255)
        limit = ((lane - base) << 24) | 0xFFFFFF
        spot = jnp.full_like(lane, -1)
        step = LANES // 2
        while step:
            probe = spot + step
            spot = jnp.where((pick(word, probe) << lift) <= limit, probe, spot)
            step //= 2
        spot = spot + 1
        found = pick(payloads[0], spot)
        for past, other in zip(later, payloads[1:]):
            found = jnp.where(past, pick(other, spot), found)
        send_ref[shard] = jnp.where(lane < start, found, 0)[:, :slots]

    def some(step, carry):
        for k in range(TOGETHER):
            place(step * TOGETHER + k)
        return carry

    lax.fori_loop(0, shards // TOGETHER, some, 0)


def prepare_kernel(
    logits_hbm, repetition_hbm, frequency_hbm, presence_hbm, plain_hbm, seen_hbm, shift_ref, rate_ref,
    logits, plain_ref, seen_ref, factors, logits_sem, factor_sem, plain_sem, seen_sem,
):
    rows, width = plain_ref.shape
    groups = rows // 8
    tiles = -(-width // LANES)
    loads = [
        pltpu.make_async_copy(
            logits_hbm.at[pl.ds(group * 8, 8)], logits.at[pl.ds(group * 8, 8)], logits_sem.at[group]
        )
        for group in range(groups)
    ]
    fetches = [
        pltpu.make_async_copy(ref, factors.at[pl.ds(k, 1)], factor_sem.at[k])
        for k, ref in enumerate((repetition_hbm, frequency_hbm, presence_hbm))
    ]
    for copy in fetches + loads:
        copy.start()
    for fetch in fetches:
        fetch.wait()
    repetition = column(factors[0:1, :], rows)
    rate_ref[...] = jnp.broadcast_to(column(factors[1:2, :], rows) * LOG2E, rate_ref.shape)
    presence = column(factors[2:3, :], rows) * LOG2E
    above, below = LOG2E / repetition, LOG2E * repetition
    stores = []
    for group in range(groups):
        loads[group].wait()
        part = slice(group * 8, group * 8 + 8)
        best = jnp.full((8, LANES), -jnp.inf, jnp.float32)
        tail = None
        for tile in range(tiles):
            size = min(LANES, width - tile * LANES)
            x = logits[part, tile * LANES : tile * LANES + size]
            if size == LANES:
                best = jnp.maximum(best, x)
            else:
                tail = jnp.max(x, axis=1, keepdims=True)
        top = jnp.max(best, axis=1, keepdims=True)
        if tail is not None:
            top = jnp.maximum(top, tail)
        shift = top * LOG2E
        shift_ref[part, :] = jnp.broadcast_to(shift, (8, shift_ref.shape[1]))
        offset = shift + presence[part]
        over, under = above[part], below[part]
        for tile in range(tiles):
            size = min(LANES, width - tile * LANES)
            columns = slice(tile * LANES, tile * LANES + size)
            x = logits[part, columns]
            plain_ref[part, columns] = x * LOG2E - shift
            seen_ref[part, columns] = x * jnp.where(x > 0, over, under) - offset
        stores.append(pltpu.make_async_copy(plain_ref.at[part], plain_hbm.at[part], plain_sem.at[group]))
        stores.append(pltpu.make_async_copy(seen_ref.at[part], seen_hbm.at[part], seen_sem.at[group]))
        for store in stores[-2:]:
            store.start()
    for store in stores:
        store.wait()


def tally_kernel(
    ordered, got_ref, plain_hbm, seen_hbm, shift_ref, rate_ref, adjusted_ref, stats_ref,
    seen_ref, dense_a, dense_b, sums_a, sums_b, trips, order, misfit, plain_sem, seen_sem,
):
    blocks, rows, _ = got_ref.shape
    width = plain_hbm.shape[1]
    groups = rows // 8
    tiles = -(-width // LANES)
    uppers = -(-(-(-width // CHUNK)) // 16) * 16
    caps = [min(cap, blocks) for cap in PROFILE]
    second = max(caps)
    dense, sums = (dense_a, dense_b), (sums_a, sums_b)

    def rows_of(group):
        return pl.ds(pl.multiple_of(group * 8, 8), 8)

    def loads(group):
        part = rows_of(group)
        return (
            pltpu.make_async_copy(plain_hbm.at[part], adjusted_ref.at[part], plain_sem.at[group]),
            pltpu.make_async_copy(seen_hbm.at[part], seen_ref.at[part], seen_sem.at[group]),
        )

    for group in range(groups):
        for copy in loads(group):
            copy.start()

    lane = lax.broadcasted_iota(jnp.int32, (8, LANES), 1)
    sub = lax.broadcasted_iota(jnp.int32, (8, LANES), 0)
    ones = jnp.ones((LANES, LANES), jnp.bfloat16)

    def keep(side, tile, word):
        local = word >> FIELD
        fields = (local // CHUNK, local & (CHUNK - 1), word & 0xFFFF)
        for k, field in enumerate(fields):
            value = field.astype(jnp.float32)
            dense[side][k, pl.ds(tile * 8, 8), :] = value * (1.0 / SCALE) if k == 2 else value

    def merge(group, side):
        words = [got_ref[block, rows_of(group), :] for block in range(blocks)]
        if not ordered:
            for block in range(blocks):
                keep(side, block, words[block])
            trips[side] = blocks
            return
        full = jnp.concatenate(words, axis=0) > 0
        count = jnp.dot(
            jnp.where(full, 1.0, 0.0).astype(jnp.bfloat16), ones, preferred_element_type=jnp.float32
        ).astype(jnp.int32)
        starts = [jnp.zeros_like(lane)]
        for block in range(blocks):
            starts.append(starts[-1] + count[block * 8 : block * 8 + 8])
        turned = [
            pick(words[block], (lane - starts[block]) & (LANES - 1))
            for block in range(blocks)
        ]
        for tile in range(blocks):
            spot = lane + tile * LANES
            value = turned[tile]
            for block in range(tile + 1, blocks):
                value = jnp.where(spot >= starts[block], turned[block], value)
            keep(side, tile, jnp.where(spot < starts[blocks], value, 0))
        have = starts[blocks]
        trips[side] = (jnp.max(have) + LANES - 1) // LANES
        across = jnp.sum(jnp.where(lane == sub, have.astype(jnp.float32), 0.0), axis=0, keepdims=True)
        across = jnp.broadcast_to(across, (8, LANES)).astype(jnp.int32)
        fewer = ((across < have) | ((across == have) & (lane < sub))) & (lane < 8)
        rank = jnp.sum(jnp.where(fewer, 1.0, 0.0), axis=1, keepdims=True)
        rank = jnp.broadcast_to(rank, (8, LANES)).astype(jnp.int32)
        cap = jnp.full_like(lane, caps[0])
        for slot in range(8):
            order[side * 8 + slot] = jnp.max(jnp.where(rank == slot, sub, 0))
            if slot and caps[slot] != caps[slot - 1]:
                cap = jnp.where(rank >= slot, caps[slot], cap)
        misfit[side] = jnp.max(jnp.where(have > cap * LANES, 1, 0))

    iota = lax.broadcasted_iota(jnp.int32, (max(CHUNK, uppers), LANES), 0).astype(jnp.float32)
    iota = iota.astype(jnp.bfloat16)
    zero = jnp.zeros((), jnp.bfloat16)
    one = jnp.ones((), jnp.bfloat16)

    def product(side, row, first_tile, count):
        def spread(k, tile, size):
            piece = dense[side][k, pl.ds(tile * 8 + row, 8, stride=0), :]
            piece = jnp.concatenate([piece, piece], axis=0).astype(jnp.bfloat16)
            return jnp.concatenate([piece] * (size // 16), axis=0)

        hot_upper, hot_lower = [], []
        for step in range(count):
            tile = first_tile + step
            hot_upper.append(jnp.where(spread(0, tile, uppers) == iota[:uppers], one, zero))
            hot_lower.append(jnp.where(spread(1, tile, CHUNK) == iota[:CHUNK], spread(2, tile, CHUNK), zero))
        return lax.dot_general(
            jnp.concatenate(hot_upper, axis=1),
            jnp.concatenate(hot_lower, axis=1),
            (((1,), (1,)), ((), ())),
            preferred_element_type=jnp.float32,
        )

    def tally_row(side, row, count):
        total = product(side, row, 0, count)
        for half in range(HALVES):
            part = total[:, half * LANES : (half + 1) * LANES]
            sums[side][half, pl.ds(row, uppers, stride=8), :] = part

    def tally_rest(side):
        def more(tile, carry):
            for row in range(8):
                total = product(side, row, tile, 1)
                for half in range(HALVES):
                    part = total[:, half * LANES : (half + 1) * LANES]
                    sums[side][half, pl.ds(row, uppers, stride=8), :] += part
            return carry

        if blocks > second:
            lax.fori_loop(second, trips[side], more, 0)

    line = lax.broadcasted_iota(jnp.int32, (8, 2 * rows), 1)
    inner = lax.broadcasted_iota(jnp.int32, (8, 2 * rows), 0)

    def place(spot, group, shift, rest):
        seq = group * 8 + inner
        return spot + jnp.where(line == seq, shift, 0.0) + jnp.where(line == seq + rows, rest, 0.0)

    def both(group, side, spot, following=None):
        for copy in loads(group):
            copy.wait()
        return either(1 - side, lambda counts: part_of(group, side, spot, counts, following))

    def either(side, run):
        plainly = [(row, second) for row in range(8)]
        if not ordered:
            return run(plainly)
        return lax.cond(
            misfit[side] > 0,
            lambda: run(plainly),
            lambda: run([(order[side * 8 + slot], caps[slot]) for slot in range(8)]),
        )

    def part_of(group, side, spot, counts, following):
        if following is not None:
            merge(following, side)
        part = rows_of(group)
        rate = rate_ref[part, :]
        totals = [jnp.zeros((8, LANES), jnp.float32)] * 4
        rest = jnp.zeros((8, 1), jnp.float32)
        share = -(-tiles // 8)
        for row in range(8):
            for tile in range(row * share, min(tiles, (row + 1) * share)):
                size = min(LANES, width - tile * LANES)
                columns = pl.ds(tile * LANES, size)
                chunk, half = divmod(tile, HALVES)
                weighted = sums[side][half, chunk * 8 : chunk * 8 + 8, :size]
                value = jnp.where(
                    weighted > 0, seen_ref[part, columns] - rate[:, :size] * weighted, adjusted_ref[part, columns]
                )
                adjusted_ref[part, columns] = value
                value = jnp.exp2(value)
                if size == LANES:
                    totals[tile % 4] = totals[tile % 4] + value
                else:
                    rest = jnp.sum(value, axis=1, keepdims=True)
            if counts:
                tally_row(1 - side, *counts[row])
        total = (totals[0] + totals[1]) + (totals[2] + totals[3])
        rest = rest + jnp.sum(total, axis=1, keepdims=True)
        return place(spot, group, shift_ref[part, :], rest)

    def renew(group, spot):
        part = rows_of(group)
        value = adjusted_ref[part, :]
        top = jnp.max(value, axis=1, keepdims=True)
        rest = jnp.sum(jnp.exp2(value - top), axis=1, keepdims=True)
        return place(spot, group, shift_ref[part, :] + top, rest)

    def begin(counts):
        merge(1, 1)
        for row, count in counts:
            tally_row(0, row, count)

    merge(0, 0)
    either(0, begin)
    tally_rest(0)

    def two(pair, spot):
        for side in range(2):
            group = pair * 2 + side
            spot = both(group, side, spot, group + 2)
            tally_rest(1 - side)
        return spot

    empty = jnp.zeros((8, 2 * rows), jnp.float32)
    spot = lax.fori_loop(0, groups // 2 - 1, two, empty)
    spot = both(groups - 2, 0, spot)
    tally_rest(1)
    for copy in loads(groups - 1):
        copy.wait()
    spot = part_of(groups - 1, 1, spot, [], None)
    spot = jnp.sum(spot, axis=0, keepdims=True)
    stats_ref[...] = jnp.broadcast_to(spot, stats_ref.shape)

    @pl.when(jnp.min(jnp.where(line[:1] < rows, 1.0, spot)) < LEAST)
    def _():
        exact = jnp.sum(lax.fori_loop(0, groups, renew, empty), axis=0, keepdims=True)
        stats_ref[...] = jnp.broadcast_to(exact, stats_ref.shape)


def finish_kernel(adjusted_ref, shift_ref, stats_ref, out_ref, result, sem):
    rows = adjusted_ref.shape[0]
    tops = stats_ref[:, :rows]
    totals = stats_ref[:, rows:]
    top = jnp.max(tops, axis=0, keepdims=True)
    total = jnp.sum(totals * jnp.exp2(tops - top), axis=0, keepdims=True)
    offset = shift_ref[:, :1] - column(top, rows)
    offset = offset * LN2 - column(jnp.log(total), rows)
    copies = []
    for group in range(rows // 8):
        part = slice(group * 8, group * 8 + 8)
        result[part, :] = adjusted_ref[part, :] * LN2 + offset[part]
        copies.append(pltpu.make_async_copy(result.at[part], out_ref.at[part], sem.at[group]))
        copies[-1].start()
    for copy in copies:
        copy.wait()


def vmem(shape, dtype):
    return pltpu.VMEM(shape, dtype)


def outside(array):
    return pltpu.with_memory_space_constraint(array, pltpu.HBM)


def body(logits, history, history_weight, lengths, repetition, frequency, presence):
    rows, width = logits.shape
    span = history.shape[1]
    shards = lax.axis_size("vocab")
    slots = max(2, 2 * span // shards)
    full = pl.BlockSpec(memory_space=pltpu.VMEM)
    away = pl.BlockSpec(memory_space=pltpu.HBM)
    ordered = slots % LANES == 0
    send = pl.pallas_call(
        functools.partial(pack_kernel, shards, slots, width),
        out_shape=vmem((shards, rows, slots), jnp.int32),
        in_specs=[away] * 3,
        out_specs=full,
        scratch_shapes=[
            vmem((rows, span), jnp.int32),
            vmem((rows, span), jnp.bfloat16),
            vmem((1, rows), jnp.int32),
            pltpu.SemaphoreType.DMA((3,)),
        ],
        compiler_params=pltpu.CompilerParams(vmem_limit_bytes=8 << 20),
        name="pack",
    )(outside(history), outside(history_weight), outside(lengths.reshape(1, rows)))
    got = lax.all_to_all(send, "vocab", split_axis=0, concat_axis=0, tiled=True)
    if ordered:
        got = got.reshape(shards, rows, slots // LANES, LANES).transpose(0, 2, 1, 3)
        got = got.reshape(-1, rows, LANES)
    else:
        got = got.transpose(1, 0, 2).reshape(rows, shards * slots)
        got = jnp.pad(got, ((0, 0), (0, -(shards * slots) % LANES)))
        got = got.reshape(rows, -1, LANES).transpose(1, 0, 2)
    got = jnp.pad(got, ((0, got.shape[0] % 2), (0, 0), (0, 0)))
    groups = rows // 8
    uppers = -(-(-(-width // CHUNK)) // 16) * 16
    wide = vmem((rows, width), jnp.float32)
    plain, seen, shift, rate = pl.pallas_call(
        prepare_kernel,
        out_shape=(
            pltpu.HBM((rows, width), jnp.float32),
            pltpu.HBM((rows, width), jnp.float32),
            vmem((rows, 2 * rows), jnp.float32),
            vmem((rows, LANES), jnp.float32),
        ),
        in_specs=[away] * 4,
        out_specs=(away, away, full, full),
        scratch_shapes=[
            wide,
            wide,
            wide,
            vmem((3, rows), jnp.float32),
            pltpu.SemaphoreType.DMA((groups,)),
            pltpu.SemaphoreType.DMA((3,)),
            pltpu.SemaphoreType.DMA((groups,)),
            pltpu.SemaphoreType.DMA((groups,)),
        ],
        compiler_params=pltpu.CompilerParams(vmem_limit_bytes=24 << 20),
        cost_estimate=pl.CostEstimate(
            flops=400 * rows * width, bytes_accessed=400 * rows * width, transcendentals=0
        ),
        name="prepare",
    )(
        outside(logits),
        outside(repetition.reshape(1, rows)),
        outside(frequency.reshape(1, rows)),
        outside(presence.reshape(1, rows)),
    )
    adjusted, stats = pl.pallas_call(
        functools.partial(tally_kernel, ordered),
        out_shape=(wide, vmem((shards, 2 * rows), jnp.float32)),
        in_specs=[full, away, away, full, full],
        out_specs=(full, full),
        scratch_shapes=[
            wide,
            *[vmem((3, got.shape[0] * 8, LANES), jnp.float32)] * 2,
            *[vmem((HALVES, uppers * 8, LANES), jnp.float32)] * 2,
            pltpu.SMEM((2,), jnp.int32),
            pltpu.SMEM((16,), jnp.int32),
            pltpu.SMEM((2,), jnp.int32),
            pltpu.SemaphoreType.DMA((groups,)),
            pltpu.SemaphoreType.DMA((groups,)),
        ],
        compiler_params=pltpu.CompilerParams(vmem_limit_bytes=16 << 20),
        name="tally",
    )(got, outside(plain), outside(seen), shift, rate)
    stats = lax.all_to_all(stats, "vocab", split_axis=0, concat_axis=0, tiled=True)
    return pl.pallas_call(
        finish_kernel,
        out_shape=jax.ShapeDtypeStruct((rows, width), jnp.float32),
        in_specs=[full] * 3,
        out_specs=away,
        scratch_shapes=[wide, pltpu.SemaphoreType.DMA((groups,))],
        compiler_params=pltpu.CompilerParams(vmem_limit_bytes=16 << 20),
        name="finish",
    )(adjusted, shift, stats)


def solution(mesh):
    return jax.shard_map(
        body,
        mesh=mesh,
        in_specs=(
            P("batch", "vocab"),
            P("batch", "vocab"),
            P("batch", "vocab"),
            P("batch"),
            P("batch"),
            P("batch"),
            P("batch"),
        ),
        out_specs=P("batch", "vocab"),
        check_vma=False,
    )
```

```python
import functools

import jax
import jax.numpy as jnp
from jax import lax
from jax.experimental import pallas as pl
from jax.experimental.pallas import tpu as pltpu
from jax.sharding import PartitionSpec as P

LANES = 128
PROFILE = (2, 2, 3, 3, 4, 4, 4, 5)
TOGETHER = 4
CHUNK = 128
HALVES = CHUNK // LANES
LOG2E = 1.4426950408889634
LN2 = 0.6931471805599453
LEAST = 1e-20
FIELD = 16
SCALE = 512.0


def pick(table, place):
    return lax.gather(
        table,
        place[:, :, None],
        lax.GatherDimensionNumbers(
            offset_dims=(),
            collapsed_slice_dims=(1,),
            start_index_map=(1,),
            operand_batching_dims=(0,),
            start_indices_batching_dims=(0,),
        ),
        slice_sizes=(1, 1),
        mode=lax.GatherScatterMode.PROMISE_IN_BOUNDS,
    )


def column(row, rows):
    wide = jnp.broadcast_to(row, (rows, rows))
    same = lax.broadcasted_iota(jnp.int32, (rows, rows), 0) == lax.broadcasted_iota(
        jnp.int32, (rows, rows), 1
    )
    return jnp.sum(jnp.where(same, wide, 0.0), axis=1, keepdims=True)


def pack_kernel(
    shards, slots, width, ids_hbm, weight_hbm, lengths_hbm, send_ref, ids_ref, weight_ref, lengths_ref, sem
):
    copies = [
        pltpu.make_async_copy(source, target, sem.at[k])
        for k, (source, target) in enumerate(
            ((ids_hbm, ids_ref), (weight_hbm, weight_ref), (lengths_hbm, lengths_ref))
        )
    ]
    for copy in copies:
        copy.start()
    for copy in copies:
        copy.wait()
    rows, span = ids_ref.shape
    tiles = span // LANES
    first = lax.axis_index("vocab") * span
    ids = ids_ref[...]
    lengths = column(lengths_ref[...].astype(jnp.float32), rows)
    positions = (lax.broadcasted_iota(jnp.int32, (rows, span), 1) + first).astype(jnp.float32)
    valid = positions < lengths
    owner = jnp.zeros_like(ids)
    for shard in range(1, shards):
        owner = owner + (ids >= shard * width).astype(jnp.int32)
    code = (weight_ref[...].astype(jnp.float32) * SCALE).astype(jnp.int32)
    payload = ((ids - owner * width) << FIELD) | code
    owner = jnp.where(valid, owner, -1)
    payloads = [payload[:, t * LANES : (t + 1) * LANES] for t in range(tiles)]
    below = lax.broadcasted_iota(jnp.int32, (LANES, LANES), 0) <= lax.broadcasted_iota(
        jnp.int32, (LANES, LANES), 1
    )
    below = jnp.where(below, 1.0, 0.0)
    low = min(tiles, 3)
    below = [(below * float(256**t)).astype(jnp.bfloat16) for t in range(low)]
    stacked = jnp.concatenate(below, axis=0)
    lane = lax.broadcasted_iota(jnp.int32, (rows, LANES), 1)
    last = jnp.full((rows, LANES), LANES - 1, jnp.int32)

    def place(shard):
        mine = jnp.where(owner == shard, 1.0, 0.0).astype(jnp.bfloat16)
        word = jnp.dot(
            mine[:, : low * LANES], stacked, preferred_element_type=jnp.float32
        ).astype(jnp.int32)
        for t in range(low, tiles):
            high = jnp.dot(
                mine[:, t * LANES : (t + 1) * LANES], below[0], preferred_element_type=jnp.float32
            )
            word = word | (high.astype(jnp.int32) << (8 * t))
        totals = pick(word, last)
        start = totals & 255
        base = jnp.zeros_like(lane)
        lift = jnp.full_like(lane, 24)
        later = []
        for t in range(1, tiles):
            past = lane >= start
            later.append(past)
            base = jnp.where(past, start, base)
            lift = jnp.where(past, 24 - 8 * t, lift)
            start = start + ((totals >> (8 * t)) & 255)
        limit = ((lane - base) << 24) | 0xFFFFFF
        spot = jnp.full_like(lane, -1)
        step = LANES // 2
        while step:
            probe = spot + step
            spot = jnp.where((pick(word, probe) << lift) <= limit, probe, spot)
            step //= 2
        spot = spot + 1
        found = pick(payloads[0], spot)
        for past, other in zip(later, payloads[1:]):
            found = jnp.where(past, pick(other, spot), found)
        send_ref[shard] = jnp.where(lane < start, found, 0)[:, :slots]

    def some(step, carry):
        for k in range(TOGETHER):
            place(step * TOGETHER + k)
        return carry

    lax.fori_loop(0, shards // TOGETHER, some, 0)


def prepare_kernel(
    logits_hbm, repetition_hbm, frequency_hbm, presence_hbm, plain_hbm, seen_hbm, shift_ref, rate_ref,
    logits, plain_ref, seen_ref, factors, logits_sem, factor_sem, plain_sem, seen_sem,
):
    rows, width = plain_ref.shape
    groups = rows // 8
    tiles = -(-width // LANES)
    loads = [
        pltpu.make_async_copy(
            logits_hbm.at[pl.ds(group * 8, 8)], logits.at[pl.ds(group * 8, 8)], logits_sem.at[group]
        )
        for group in range(groups)
    ]
    fetches = [
        pltpu.make_async_copy(ref, factors.at[pl.ds(k, 1)], factor_sem.at[k])
        for k, ref in enumerate((repetition_hbm, frequency_hbm, presence_hbm))
    ]
    for copy in fetches + loads:
        copy.start()
    for fetch in fetches:
        fetch.wait()
    repetition = column(factors[0:1, :], rows)
    rate_ref[...] = jnp.broadcast_to(column(factors[1:2, :], rows) * LOG2E, rate_ref.shape)
    presence = column(factors[2:3, :], rows) * LOG2E
    above, below = LOG2E / repetition, LOG2E * repetition
    stores = []
    for group in range(groups):
        loads[group].wait()
        part = slice(group * 8, group * 8 + 8)
        bests = [jnp.full((8, LANES), -jnp.inf, jnp.float32)] * 8
        tail = None
        for tile in range(tiles):
            size = min(LANES, width - tile * LANES)
            x = logits[part, tile * LANES : tile * LANES + size]
            if size == LANES:
                bests[tile % 8] = jnp.maximum(bests[tile % 8], x)
            else:
                tail = jnp.max(x, axis=1, keepdims=True)
        top = jnp.max(functools.reduce(jnp.maximum, bests), axis=1, keepdims=True)
        if tail is not None:
            top = jnp.maximum(top, tail)
        shift = top * LOG2E
        shift_ref[part, :] = jnp.broadcast_to(shift, (8, shift_ref.shape[1]))
        offset = shift + presence[part]
        over, under = above[part], below[part]
        for tile in range(tiles):
            size = min(LANES, width - tile * LANES)
            columns = slice(tile * LANES, tile * LANES + size)
            x = logits[part, columns]
            plain_ref[part, columns] = x * LOG2E - shift
            seen_ref[part, columns] = x * jnp.where(x > 0, over, under) - offset
        stores.append(pltpu.make_async_copy(plain_ref.at[part], plain_hbm.at[part], plain_sem.at[group]))
        stores.append(pltpu.make_async_copy(seen_ref.at[part], seen_hbm.at[part], seen_sem.at[group]))
        for store in stores[-2:]:
            store.start()
    for store in stores:
        store.wait()


def tally_kernel(
    ordered, got_ref, plain_hbm, seen_hbm, shift_ref, rate_ref, adjusted_ref, stats_ref,
    seen_ref, dense_a, dense_b, sums_a, sums_b, trips, order, misfit, plain_sem, seen_sem,
):
    blocks, rows, _ = got_ref.shape
    width = plain_hbm.shape[1]
    groups = rows // 8
    tiles = -(-width // LANES)
    uppers = -(-(-(-width // CHUNK)) // 16) * 16
    caps = [min(cap, blocks) for cap in PROFILE]
    second = max(caps)
    dense, sums = (dense_a, dense_b), (sums_a, sums_b)

    def rows_of(group):
        return pl.ds(pl.multiple_of(group * 8, 8), 8)

    def loads(group):
        part = rows_of(group)
        return (
            pltpu.make_async_copy(plain_hbm.at[part], adjusted_ref.at[part], plain_sem.at[group]),
            pltpu.make_async_copy(seen_hbm.at[part], seen_ref.at[part], seen_sem.at[group]),
        )

    for group in range(groups):
        for copy in loads(group):
            copy.start()

    lane = lax.broadcasted_iota(jnp.int32, (8, LANES), 1)
    sub = lax.broadcasted_iota(jnp.int32, (8, LANES), 0)
    ones = jnp.ones((LANES, LANES), jnp.bfloat16)

    def keep(side, tile, word):
        local = word >> FIELD
        fields = (local // CHUNK, local & (CHUNK - 1), word & 0xFFFF)
        for k, field in enumerate(fields):
            value = field.astype(jnp.float32)
            dense[side][k, pl.ds(tile * 8, 8), :] = value * (1.0 / SCALE) if k == 2 else value

    def merge(group, side):
        words = [got_ref[block, rows_of(group), :] for block in range(blocks)]
        if not ordered:
            for block in range(blocks):
                keep(side, block, words[block])
            trips[side] = blocks
            return
        full = jnp.concatenate(words, axis=0) > 0
        count = jnp.dot(
            jnp.where(full, 1.0, 0.0).astype(jnp.bfloat16), ones, preferred_element_type=jnp.float32
        ).astype(jnp.int32)
        starts = [jnp.zeros_like(lane)]
        for block in range(blocks):
            starts.append(starts[-1] + count[block * 8 : block * 8 + 8])
        turned = [
            pick(words[block], (lane - starts[block]) & (LANES - 1))
            for block in range(blocks)
        ]
        for tile in range(blocks):
            spot = lane + tile * LANES
            value = turned[tile]
            for block in range(tile + 1, blocks):
                value = jnp.where(spot >= starts[block], turned[block], value)
            keep(side, tile, jnp.where(spot < starts[blocks], value, 0))
        have = starts[blocks]
        trips[side] = (jnp.max(have) + LANES - 1) // LANES
        across = jnp.sum(jnp.where(lane == sub, have.astype(jnp.float32), 0.0), axis=0, keepdims=True)
        across = jnp.broadcast_to(across, (8, LANES)).astype(jnp.int32)
        fewer = ((across < have) | ((across == have) & (lane < sub))) & (lane < 8)
        rank = jnp.sum(jnp.where(fewer, 1.0, 0.0), axis=1, keepdims=True)
        rank = jnp.broadcast_to(rank, (8, LANES)).astype(jnp.int32)
        cap = jnp.full_like(lane, caps[0])
        for slot in range(8):
            order[side * 8 + slot] = jnp.max(jnp.where(rank == slot, sub, 0))
            if slot and caps[slot] != caps[slot - 1]:
                cap = jnp.where(rank >= slot, caps[slot], cap)
        misfit[side] = jnp.max(jnp.where(have > cap * LANES, 1, 0))

    iota = lax.broadcasted_iota(jnp.int32, (max(CHUNK, uppers), LANES), 0).astype(jnp.float32)
    iota = iota.astype(jnp.bfloat16)
    zero = jnp.zeros((), jnp.bfloat16)
    one = jnp.ones((), jnp.bfloat16)

    def product(side, row, first_tile, count):
        def spread(k, tile, size):
            piece = dense[side][k, pl.ds(tile * 8 + row, 8, stride=0), :]
            piece = jnp.concatenate([piece, piece], axis=0).astype(jnp.bfloat16)
            return jnp.concatenate([piece] * (size // 16), axis=0)

        hot_upper, hot_lower = [], []
        for step in range(count):
            tile = first_tile + step
            hot_upper.append(jnp.where(spread(0, tile, uppers) == iota[:uppers], one, zero))
            hot_lower.append(jnp.where(spread(1, tile, CHUNK) == iota[:CHUNK], spread(2, tile, CHUNK), zero))
        return lax.dot_general(
            jnp.concatenate(hot_upper, axis=1),
            jnp.concatenate(hot_lower, axis=1),
            (((1,), (1,)), ((), ())),
            preferred_element_type=jnp.float32,
        )

    def tally_row(side, row, count):
        total = product(side, row, 0, count)
        for half in range(HALVES):
            part = total[:, half * LANES : (half + 1) * LANES]
            sums[side][half, pl.ds(row, uppers, stride=8), :] = part

    def tally_rest(side):
        def more(tile, carry):
            for row in range(8):
                total = product(side, row, tile, 1)
                for half in range(HALVES):
                    part = total[:, half * LANES : (half + 1) * LANES]
                    sums[side][half, pl.ds(row, uppers, stride=8), :] += part
            return carry

        if blocks > second:
            lax.fori_loop(second, trips[side], more, 0)

    line = lax.broadcasted_iota(jnp.int32, (8, 2 * rows), 1)
    inner = lax.broadcasted_iota(jnp.int32, (8, 2 * rows), 0)

    def place(spot, group, shift, rest):
        seq = group * 8 + inner
        return spot + jnp.where(line == seq, shift, 0.0) + jnp.where(line == seq + rows, rest, 0.0)

    def both(group, side, spot, following=None):
        for copy in loads(group):
            copy.wait()
        return either(1 - side, lambda counts: part_of(group, side, spot, counts, following))

    def either(side, run):
        plainly = [(row, second) for row in range(8)]
        if not ordered:
            return run(plainly)
        return lax.cond(
            misfit[side] > 0,
            lambda: run(plainly),
            lambda: run([(order[side * 8 + slot], caps[slot]) for slot in range(8)]),
        )

    def part_of(group, side, spot, counts, following):
        if following is not None:
            merge(following, side)
        part = rows_of(group)
        rate = rate_ref[part, :]
        totals = [jnp.zeros((8, LANES), jnp.float32)] * 4
        rest = jnp.zeros((8, 1), jnp.float32)
        share = -(-tiles // 8)
        for row in range(8):
            for tile in range(row * share, min(tiles, (row + 1) * share)):
                size = min(LANES, width - tile * LANES)
                columns = pl.ds(tile * LANES, size)
                chunk, half = divmod(tile, HALVES)
                weighted = sums[side][half, chunk * 8 : chunk * 8 + 8, :size]
                value = jnp.where(
                    weighted > 0, seen_ref[part, columns] - rate[:, :size] * weighted, adjusted_ref[part, columns]
                )
                adjusted_ref[part, columns] = value
                value = jnp.exp2(value)
                if size == LANES:
                    totals[tile % 4] = totals[tile % 4] + value
                else:
                    rest = jnp.sum(value, axis=1, keepdims=True)
            if counts:
                tally_row(1 - side, *counts[row])
        total = (totals[0] + totals[1]) + (totals[2] + totals[3])
        rest = rest + jnp.sum(total, axis=1, keepdims=True)
        return place(spot, group, shift_ref[part, :], rest)

    def renew(group, spot):
        part = rows_of(group)
        value = adjusted_ref[part, :]
        top = jnp.max(value, axis=1, keepdims=True)
        rest = jnp.sum(jnp.exp2(value - top), axis=1, keepdims=True)
        return place(spot, group, shift_ref[part, :] + top, rest)

    def begin(counts):
        merge(1, 1)
        for row, count in counts:
            tally_row(0, row, count)

    merge(0, 0)
    either(0, begin)
    tally_rest(0)

    def two(pair, spot):
        for side in range(2):
            group = pair * 2 + side
            spot = both(group, side, spot, group + 2)
            tally_rest(1 - side)
        return spot

    empty = jnp.zeros((8, 2 * rows), jnp.float32)
    spot = lax.fori_loop(0, groups // 2 - 1, two, empty)
    spot = both(groups - 2, 0, spot)
    tally_rest(1)
    for copy in loads(groups - 1):
        copy.wait()
    spot = part_of(groups - 1, 1, spot, [], None)
    spot = jnp.sum(spot, axis=0, keepdims=True)
    stats_ref[...] = jnp.broadcast_to(spot, stats_ref.shape)

    @pl.when(jnp.min(jnp.where(line[:1] < rows, 1.0, spot)) < LEAST)
    def _():
        exact = jnp.sum(lax.fori_loop(0, groups, renew, empty), axis=0, keepdims=True)
        stats_ref[...] = jnp.broadcast_to(exact, stats_ref.shape)


def finish_kernel(adjusted_ref, shift_ref, stats_ref, out_ref, result, sem):
    rows = adjusted_ref.shape[0]
    tops = stats_ref[:, :rows]
    totals = stats_ref[:, rows:]
    top = jnp.max(tops, axis=0, keepdims=True)
    total = jnp.sum(totals * jnp.exp2(tops - top), axis=0, keepdims=True)
    offset = shift_ref[:, :1] - column(top, rows)
    offset = offset * LN2 - column(jnp.log(total), rows)
    copies = []
    for group in range(rows // 8):
        part = slice(group * 8, group * 8 + 8)
        result[part, :] = adjusted_ref[part, :] * LN2 + offset[part]
        copies.append(pltpu.make_async_copy(result.at[part], out_ref.at[part], sem.at[group]))
        copies[-1].start()
    for copy in copies:
        copy.wait()


def vmem(shape, dtype):
    return pltpu.VMEM(shape, dtype)


def outside(array):
    return pltpu.with_memory_space_constraint(array, pltpu.HBM)


def body(logits, history, history_weight, lengths, repetition, frequency, presence):
    rows, width = logits.shape
    span = history.shape[1]
    shards = lax.axis_size("vocab")
    slots = max(2, 2 * span // shards)
    full = pl.BlockSpec(memory_space=pltpu.VMEM)
    away = pl.BlockSpec(memory_space=pltpu.HBM)
    ordered = slots % LANES == 0
    send = pl.pallas_call(
        functools.partial(pack_kernel, shards, slots, width),
        out_shape=vmem((shards, rows, slots), jnp.int32),
        in_specs=[away] * 3,
        out_specs=full,
        scratch_shapes=[
            vmem((rows, span), jnp.int32),
            vmem((rows, span), jnp.bfloat16),
            vmem((1, rows), jnp.int32),
            pltpu.SemaphoreType.DMA((3,)),
        ],
        compiler_params=pltpu.CompilerParams(vmem_limit_bytes=8 << 20),
        name="pack",
    )(outside(history), outside(history_weight), outside(lengths.reshape(1, rows)))
    got = lax.all_to_all(send, "vocab", split_axis=0, concat_axis=0, tiled=True)
    if ordered:
        got = got.reshape(shards, rows, slots // LANES, LANES).transpose(0, 2, 1, 3)
        got = got.reshape(-1, rows, LANES)
    else:
        got = got.transpose(1, 0, 2).reshape(rows, shards * slots)
        got = jnp.pad(got, ((0, 0), (0, -(shards * slots) % LANES)))
        got = got.reshape(rows, -1, LANES).transpose(1, 0, 2)
    got = jnp.pad(got, ((0, got.shape[0] % 2), (0, 0), (0, 0)))
    groups = rows // 8
    uppers = -(-(-(-width // CHUNK)) // 16) * 16
    wide = vmem((rows, width), jnp.float32)
    plain, seen, shift, rate = pl.pallas_call(
        prepare_kernel,
        out_shape=(
            pltpu.HBM((rows, width), jnp.float32),
            pltpu.HBM((rows, width), jnp.float32),
            vmem((rows, 2 * rows), jnp.float32),
            vmem((rows, LANES), jnp.float32),
        ),
        in_specs=[away] * 4,
        out_specs=(away, away, full, full),
        scratch_shapes=[
            wide,
            wide,
            wide,
            vmem((3, rows), jnp.float32),
            pltpu.SemaphoreType.DMA((groups,)),
            pltpu.SemaphoreType.DMA((3,)),
            pltpu.SemaphoreType.DMA((groups,)),
            pltpu.SemaphoreType.DMA((groups,)),
        ],
        compiler_params=pltpu.CompilerParams(vmem_limit_bytes=24 << 20),
        cost_estimate=pl.CostEstimate(
            flops=400 * rows * width, bytes_accessed=400 * rows * width, transcendentals=0
        ),
        name="prepare",
    )(
        outside(logits),
        outside(repetition.reshape(1, rows)),
        outside(frequency.reshape(1, rows)),
        outside(presence.reshape(1, rows)),
    )
    adjusted, stats = pl.pallas_call(
        functools.partial(tally_kernel, ordered),
        out_shape=(wide, vmem((shards, 2 * rows), jnp.float32)),
        in_specs=[full, away, away, full, full],
        out_specs=(full, full),
        scratch_shapes=[
            wide,
            *[vmem((3, got.shape[0] * 8, LANES), jnp.float32)] * 2,
            *[vmem((HALVES, uppers * 8, LANES), jnp.float32)] * 2,
            pltpu.SMEM((2,), jnp.int32),
            pltpu.SMEM((16,), jnp.int32),
            pltpu.SMEM((2,), jnp.int32),
            pltpu.SemaphoreType.DMA((groups,)),
            pltpu.SemaphoreType.DMA((groups,)),
        ],
        compiler_params=pltpu.CompilerParams(vmem_limit_bytes=16 << 20),
        name="tally",
    )(got, outside(plain), outside(seen), shift, rate)
    stats = lax.all_to_all(stats, "vocab", split_axis=0, concat_axis=0, tiled=True)
    return pl.pallas_call(
        finish_kernel,
        out_shape=jax.ShapeDtypeStruct((rows, width), jnp.float32),
        in_specs=[full] * 3,
        out_specs=away,
        scratch_shapes=[wide, pltpu.SemaphoreType.DMA((groups,))],
        compiler_params=pltpu.CompilerParams(vmem_limit_bytes=16 << 20),
        name="finish",
    )(adjusted, shift, stats)


def solution(mesh):
    return jax.shard_map(
        body,
        mesh=mesh,
        in_specs=(
            P("batch", "vocab"),
            P("batch", "vocab"),
            P("batch", "vocab"),
            P("batch"),
            P("batch"),
            P("batch"),
            P("batch"),
        ),
        out_specs=P("batch", "vocab"),
        check_vma=False,
    )
```
